128 devices in a mesh: ctx: 32 (over y, z, core), tp: 4 (over x).
Axes of the slice: x: 4, y: 4, z: 4, core: 2. Of those that a mesh axis runs over, the one named last changes fastest.
Arguments:
- query: bfloat16 [16384, 6144], P('ctx', 'tp'), may hold values from -6 to 6
- key_in: bfloat16 [16384, 6144], P('ctx', 'tp'), may hold values from -6 to 6
- value_in: bfloat16 [16384, 6144], P('ctx', 'tp'), may hold values from -6 to 6
- dout: bfloat16 [16384, 6144], P('ctx', 'tp'), may hold values from -0.5 to 0.5
- summary_offset: int32 [4], replicated, may hold values from 0 to 31
Outputs:
- grad_query: bfloat16 [16384, 6144], P(('ctx', 'tp'))
- grad_key: bfloat16 [16384, 6144], P(('ctx', 'tp'))
- grad_value: bfloat16 [16384, 6144], P(('ctx', 'tp'))
The draws below stay inside these ranges and needn't reach their ends.
Inputs may be any that keep to these rules, and one draw needn't show every extreme that they name: Summary block s is block s * 32 + summary_offset[s].
All inputs are finite; a program needn't handle non-finite values.
Results may differ from the reference program's by a relative error of at most 0.014.
Values may be sent and summed in bfloat16 or wider, within the bound.
No kernel may reach another device: no remote copies, remote signals or barrier semaphores. Data moves between devices by JAX's collectives and lax.ppermute only.
A program may use at most 128 MiB of HBM per device.

```python
import jax
import jax.numpy as jnp
from jax import lax

HEADS = 48
HDIM = 128
BLOCK = 128
BAND = 8
STRIDE = 32
SEQ = 16384
NSUM = 4


def base_draw(key, salt):
    width = HEADS * HDIM
    values = jnp.clip(jax.random.normal(jax.random.fold_in(key, salt), (SEQ, width), jnp.float32), -6.0, 6.0)
    return values


def draw_query(key, part):
    values = base_draw(key, 11)
    return values.astype(jnp.bfloat16)


def draw_key_in(key, part):
    values = base_draw(key, 12)
    return values.astype(jnp.bfloat16)


def plant(drawn, own_key, low, top_value):
    longest = drawn.shape.index(max(drawn.shape))
    spots = []
    for shift in (0, 1):
        where = [jax.random.randint(jax.random.fold_in(own_key, axis), (), 0, length) for axis, length in enumerate(drawn.shape)]
        where[longest] = (where[longest] + shift) % drawn.shape[longest]
        spots.append(tuple(where))
    return drawn.at[spots[0]].set(low).at[spots[1]].set(top_value)


def block_levels(own_key, dims, cuts, smallest, high):
    def one(axis_at, parts):
        heights = jax.random.uniform(jax.random.fold_in(jax.random.fold_in(own_key, 6), axis_at), (parts,), jnp.float32, smallest / len(cuts), high / len(cuts))
        return jnp.repeat(jnp.exp(heights), dims[axis_at] // parts).reshape((-1,) + (1,) * (len(dims) - axis_at - 1))

    gain = one(*cuts[0])
    for cut in cuts[1:]:
        gain = gain * one(*cut)
    return gain


def gaussian(rng, extent, scale, bound, cuts=(), kind=jnp.bfloat16):
    factor_of = block_levels(rng, extent, cuts, -0.22, 0.18) if cuts else 1.0
    entries = jax.random.normal(rng, extent, jnp.float32) * scale * factor_of
    return jnp.minimum(jnp.maximum(entries, -bound), bound).astype(kind)


def setup_inputs(seed: int = 0) -> dict:
    key_of = jax.random.split(jax.random.key(seed), 6)
    return {
        "query": draw_query(jax.random.fold_in(key_of[5], 71), 0),
        "key_in": draw_key_in(jax.random.fold_in(key_of[5], 71), 0),
        "value_in": gaussian(key_of[2], (SEQ, HEADS * HDIM), 1.0, 6.0, ((0, 32), (1, 4))),
        "dout": gaussian(key_of[3], (SEQ, HEADS * HDIM), HDIM ** -0.5, 0.5, ((0, 32), (1, 4))),
        "summary_offset": plant(jax.random.randint(key_of[4], (NSUM,), 0, STRIDE), jax.random.fold_in(key_of[4], 1), 0, STRIDE - 1).astype(jnp.int32),
    }


def reference(query, key_in, value_in, dout, summary_offset):
    seq, width = query.shape
    heads = width // HDIM
    blocks = seq // BLOCK
    scale = HDIM ** -0.5
    groups = (jnp.arange(NSUM, dtype=jnp.int32) * STRIDE + summary_offset).astype(jnp.int32)
    key_blocks = key_in.reshape(blocks, BLOCK, width)
    value_blocks = value_in.reshape(blocks, BLOCK, width)
    within = jnp.arange(BLOCK, dtype=jnp.int32)
    nkeys = BAND + NSUM

    def step(carry, qblock):
        grad_k, grad_v = carry
        band = qblock - (BAND - 1) + jnp.arange(BAND, dtype=jnp.int32)
        valid = jnp.concatenate([band >= 0, groups < qblock - (BAND - 1)])
        index = jnp.concatenate([jnp.maximum(band, 0), groups]).astype(jnp.int32)
        keys = key_blocks[index].reshape(nkeys * BLOCK, heads, HDIM).astype(jnp.float32)
        values = value_blocks[index].reshape(nkeys * BLOCK, heads, HDIM).astype(jnp.float32)
        start = (qblock * BLOCK).astype(jnp.int32)
        rows_q = lax.dynamic_slice_in_dim(query, start, BLOCK, 0).reshape(BLOCK, heads, HDIM).astype(jnp.float32)
        rows_do = lax.dynamic_slice_in_dim(dout, start, BLOCK, 0).reshape(BLOCK, heads, HDIM).astype(jnp.float32)
        key_tok = (index[:, None] * BLOCK + within[None, :]).reshape(-1)
        query_tok = start + within
        allowed = jnp.repeat(valid, BLOCK)[None, :] & (key_tok[None, :] <= query_tok[:, None])
        allowed = allowed[None, :, :]
        scores = jnp.einsum("qhd,khd->hqk", rows_q, keys) * scale
        top = jnp.max(jnp.where(allowed, scores, -jnp.inf), axis=2, keepdims=True)
        total = jnp.sum(jnp.where(allowed, jnp.exp(scores - top), 0.0), axis=2, keepdims=True)
        lse = top + jnp.log(total)
        prob = jnp.where(allowed, jnp.exp(scores - lse), 0.0)
        dprob = jnp.einsum("qhd,khd->hqk", rows_do, values)
        delta = jnp.sum(prob * dprob, axis=2, keepdims=True)
        dscore = (prob * (dprob - delta)).astype(jnp.bfloat16).astype(jnp.float32)
        prob_low = prob.astype(jnp.bfloat16).astype(jnp.float32)
        grad_q = (jnp.einsum("hqk,khd->qhd", dscore, keys) * scale).astype(jnp.bfloat16)
        part_k = jnp.einsum("hqk,qhd->khd", dscore, rows_q) * scale
        part_v = jnp.einsum("hqk,qhd->khd", prob_low, rows_do)
        grad_k = grad_k.at[index].add(part_k.reshape(nkeys, BLOCK, width))
        grad_v = grad_v.at[index].add(part_v.reshape(nkeys, BLOCK, width))
        return (grad_k, grad_v), grad_q.reshape(BLOCK, width)

    empty = jnp.zeros((blocks, BLOCK, width), jnp.float32)
    (grad_k, grad_v), grad_q = lax.scan(step, (empty, empty), jnp.arange(blocks, dtype=jnp.int32))
    return (grad_q.reshape(seq, width), grad_k.reshape(seq, width).astype(jnp.bfloat16), grad_v.reshape(seq, width).astype(jnp.bfloat16))
```

```python
import functools
import math

import jax
import jax.numpy as jnp
from jax import lax
from jax.experimental import pallas as pl
from jax.experimental.pallas import tpu as pltpu
from jax.sharding import PartitionSpec as P


HDIM = 128
BLOCK = 128
BAND = 8
STRIDE = 32
CHIP_BLOCKS = 8
HALO = (BAND - 1) * BLOCK
OWN = CHIP_BLOCKS * BLOCK
EXT = HALO + OWN
TILE = 256
NSUM = 4
SPAN = 9
ROWS = (SPAN + NSUM) * BLOCK
NEG = -1e30
SIZES = (2, 2, 2)
BATCHES = ((0, 1), (2,))
CHIPS = 16
SIDE = 4
SCALE = HDIM**-0.5
LOG2E = math.log2(math.e)
BF16 = jnp.bfloat16
F32 = jnp.float32


def ring(step):
    return [(2 * c + k, 2 * ((c + step) % CHIPS) + k) for c in range(CHIPS) for k in range(2)]


def along_z(step):
    return [
        (2 * (y * SIDE + z) + k, 2 * (y * SIDE + (z + step) % SIDE) + k)
        for y in range(SIDE)
        for z in range(SIDE)
        for k in range(2)
    ]


def along_y(step):
    return [
        (2 * (y * SIDE + z) + k, 2 * ((y + step) % SIDE * SIDE + z) + k)
        for y in range(SIDE)
        for z in range(SIDE)
        for k in range(2)
    ]


SWAP = [(d, d ^ 1) for d in range(2 * CHIPS)]


def along_x(step):
    return [(x, (x + step) % SIDE) for x in range(SIDE)]


def params(**kw):
    return pltpu.CompilerParams(vmem_limit_bytes=56 * 1024 * 1024, **kw)


def cost(flops, nbytes):
    return pl.CostEstimate(flops=flops, bytes_accessed=nbytes, transcendentals=0)


def whole(shape):
    return pl.BlockSpec(shape, lambda *_: (0,) * len(shape))


def pack_kernel(sc, off, *refs):
    ins, (own, oth) = refs[:8], refs[8:]
    for n in range(4):
        own[n] = ins[2 * n][...]
        oth[n] = ins[2 * n + 1][...]


def pack(sc, off, arrays, base, heads, width):
    rows = arrays[0].shape[0]
    half = width // HDIM // 2
    chunk = 256
    cols = heads * HDIM
    specs, args = [], []
    for array in arrays:
        for other in (0, 1):
            specs.append(
                pl.BlockSpec(
                    (chunk, cols),
                    lambda i, sc, off, other=other: (
                        i,
                        jnp.abs(sc[1] - other) * (half // heads) + base // heads,
                    ),
                )
            )
            args.append(array)
    out = pl.BlockSpec((4, chunk, cols), lambda i, sc, off: (0, i, 0))
    shape = jax.ShapeDtypeStruct((4, rows, cols), BF16)
    return pl.pallas_call(
        pack_kernel,
        grid_spec=pltpu.PrefetchScalarGridSpec(
            num_scalar_prefetch=2,
            grid=(rows // chunk,),
            in_specs=specs,
            out_specs=[out, out],
        ),
        out_shape=[shape, shape],
        compiler_params=params(),
        cost_estimate=cost(0, 16 * rows * cols * 2),
        name="pack",
    )(sc, off, *args)


def halo_kernel(sc, off, own, recv, out):
    lo = OWN // 2

    def fill(first, second):
        out[:, : lo - BLOCK] = first[:, BLOCK:]
        out[:, lo - BLOCK :] = second[...]

    pl.when(sc[1] == 0)(lambda: fill(own, recv))
    pl.when(sc[1] == 1)(lambda: fill(recv, own))


def halo_of(sc, off, own, recv):
    width = own.shape[2]
    spec = pl.BlockSpec((1, OWN // 2, width), lambda i, sc, off: (2 + i, 0, 0))
    return pl.pallas_call(
        halo_kernel,
        grid_spec=pltpu.PrefetchScalarGridSpec(
            num_scalar_prefetch=2,
            grid=(2,),
            in_specs=[spec, spec],
            out_specs=pl.BlockSpec((1, HALO, width), lambda i, sc, off: (i, 0, 0)),
        ),
        out_shape=jax.ShapeDtypeStruct((2, HALO, width), BF16),
        compiler_params=params(),
        cost_estimate=cost(0, 8 * OWN * width * 2),
        name="halo",
    )(sc, off, own, recv)


def candidate_kernel(sc, off, key, value, own, oth):
    half = own.shape[2]
    for n, ref in enumerate((key, value)):
        own[n] = ref[:, pl.ds(pl.multiple_of(sc[1] * half, HDIM), half)]
        oth[n] = ref[:, pl.ds(pl.multiple_of((1 - sc[1]) * half, HDIM), half)]


def candidate(sc, off, key, value):
    width = key.shape[1]
    spec = pl.BlockSpec((BLOCK, width), lambda i, sc, off: (off[sc[2]] & 3, 0))
    shape = (2, BLOCK, width // 2)
    return pl.pallas_call(
        candidate_kernel,
        grid_spec=pltpu.PrefetchScalarGridSpec(
            num_scalar_prefetch=2, grid=(1,), in_specs=[spec] * 2, out_specs=[whole(shape)] * 2
        ),
        out_shape=[jax.ShapeDtypeStruct(shape, BF16)] * 2,
        compiler_params=params(),
        cost_estimate=cost(0, 8 * BLOCK * width),
        name="candidate",
    )(sc, off, key, value)


def pieces_kernel(sc, off, own, recv, *outs):
    piece = BLOCK // SIDE
    mine = ((off[sc[2]] & 7) >> 2) == sc[1]
    for step in range(SIDE):
        row = pl.multiple_of(((sc[3] + step) & 3) * piece, piece)

        def put(ref, out=outs[step], row=row):
            out[...] = ref[:, pl.ds(row, piece), :]

        pl.when(mine)(functools.partial(put, own))
        pl.when(jnp.logical_not(mine))(functools.partial(put, recv))


def pieces_of(sc, off, own, recv):
    shape = (2, BLOCK // SIDE, own.shape[2])
    return pl.pallas_call(
        pieces_kernel,
        grid_spec=pltpu.PrefetchScalarGridSpec(
            num_scalar_prefetch=2,
            grid=(1,),
            in_specs=[whole(own.shape)] * 2,
            out_specs=[whole(shape)] * SIDE,
        ),
        out_shape=[jax.ShapeDtypeStruct(shape, BF16)] * SIDE,
        compiler_params=params(),
        cost_estimate=cost(0, 8 * own.size),
        name="pieces",
    )(sc, off, own, recv)


def gather_kernel(sc, off, *refs):
    out = refs[SIDE]
    piece = BLOCK // SIDE
    for step in range(SIDE):
        row = pl.multiple_of(((sc[3] + SIDE - step) % SIDE) * piece, piece)
        out[:, pl.ds(row, piece), :] = refs[step][...]


def gather(sc, off, pieces):
    shape = pieces[0].shape
    full = (2, BLOCK, shape[2])
    return pl.pallas_call(
        gather_kernel,
        grid_spec=pltpu.PrefetchScalarGridSpec(
            num_scalar_prefetch=2, grid=(1,), in_specs=[whole(shape)] * SIDE, out_specs=whole(full)
        ),
        out_shape=jax.ShapeDtypeStruct(full, BF16),
        compiler_params=params(),
        cost_estimate=cost(0, 4 * BLOCK * shape[2] * 2),
        name="gather",
    )(sc, off, *pieces)


def fold(x, op):
    return op(x.reshape(x.shape[0] // 8, 8, x.shape[1]), axis=0)


def spread(x):
    return x.reshape(x.shape[0] // 8, 8, x.shape[1])


def dot_nt(a, b):
    return lax.dot_general(a, b, (((1,), (1,)), ((), ())), preferred_element_type=F32)


def dot_nn(a, b):
    return lax.dot_general(a, b, (((1,), (0,)), ((), ())), preferred_element_type=F32)


def attn_kernel(sc, off, own, recv, halo, s0, s1, s2, s3, dq, dkv, dh, ds_out, *scratch):
    kx, vx, qs, dos, kxt, acc_k, acc_v, xs, dps, dsb = scratch
    core, chip, y = sc[1], sc[0], sc[2]
    half = OWN // 2
    mine = pl.multiple_of(core * half, half)
    theirs = pl.multiple_of((1 - core) * half, half)
    qs[pl.ds(mine, half), :] = own[0]
    qs[pl.ds(theirs, half), :] = recv[0]
    dos[pl.ds(mine, half), :] = own[1]
    dos[pl.ds(theirs, half), :] = recv[1]
    for buf, n in ((kx, 0), (vx, 1)):
        buf[0:HALO, :] = halo[n]
        buf[pl.ds(HALO + mine, half), :] = own[2 + n]
        buf[pl.ds(HALO + theirs, half), :] = recv[2 + n]
        for s, part in enumerate((s0, s1, s2, s3)):
            buf[EXT + s * BLOCK : EXT + (s + 1) * BLOCK, :] = part[n]
    kxt[...] = kx[...].T
    acc_k[...] = jnp.zeros_like(acc_k)
    acc_v[...] = jnp.zeros_like(acc_v)
    row = lax.broadcasted_iota(jnp.int32, (BLOCK, TILE), 0)
    col = lax.broadcasted_iota(jnp.int32, (BLOCK, TILE), 1)
    first = lax.broadcasted_iota(jnp.int32, (1, TILE), 1) < BLOCK

    def tile(t, _):
        base = pl.multiple_of(t * TILE, TILE)
        q_t = qs[pl.ds(base, TILE), :]
        do_t = dos[pl.ds(base, TILE), :]

        def rows_of(j):
            if j < SPAN:
                return pl.multiple_of(base + j * BLOCK, BLOCK)
            return EXT + (j - SPAN) * BLOCK

        m8 = jnp.full((8, TILE), NEG, F32)
        l8 = jnp.zeros((8, TILE), F32)
        d8 = jnp.zeros((8, TILE), F32)
        tops = []
        for j in range(SPAN + NSUM):
            span = slice(j * BLOCK, (j + 1) * BLOCK)
            at = pl.ds(rows_of(j), BLOCK)
            x = dot_nt(kx[at, :], q_t) * (SCALE * LOG2E)
            if j < BAND - 1:
                outside = (chip == 0) & (2 * t + j < BAND - 1)
                x = x + jnp.where(outside, NEG, 0.0)
            if j == 0:
                x = jnp.where(first, x, NEG)
            if j == BAND - 1:
                x = jnp.where(row <= col, x, NEG)
            if j == BAND:
                x = jnp.where(row + BLOCK <= col, x, NEG)
            if j >= SPAN:
                slot = (y + NSUM - (j - SPAN)) & 3
                g = slot * STRIDE + off[slot]
                block = chip * CHIP_BLOCKS + 2 * t - (BAND - 1)
                b0 = jnp.where(g < block, 0.0, NEG)
                b1 = jnp.where(g < block + 1, 0.0, NEG)
                x = x + jnp.where(first, b0, b1)
            dp = dot_nt(vx[at, :], do_t)
            top = jnp.maximum(m8, fold(x, jnp.max))
            fade = jnp.exp2(m8 - top)
            p = jnp.exp2(spread(x) - top[None])
            l8 = l8 * fade + jnp.sum(p, axis=0)
            d8 = d8 * fade + jnp.sum(p * spread(dp), axis=0)
            xs[span, :] = p.reshape(BLOCK, TILE)
            dps[span, :] = dp
            m8 = top
            tops.append(top)
        m = jnp.max(m8, axis=0, keepdims=True)
        rest = jnp.exp2(m8 - m)
        inv = 1.0 / jnp.sum(l8 * rest, axis=0, keepdims=True)
        delta = jnp.sum(d8 * rest, axis=0, keepdims=True) * inv
        for j in range(SPAN + NSUM):
            span = slice(j * BLOCK, (j + 1) * BLOCK)
            at = pl.ds(rows_of(j), BLOCK)
            factor = jnp.exp2(tops[j] - m) * inv
            p = (spread(xs[span, :]) * factor[None]).reshape(BLOCK, TILE)
            ds = (p * (dps[span, :] - delta)).astype(BF16)
            dsb[span, :] = ds
            acc_v[at, :] += dot_nn(p.astype(BF16), do_t)
            acc_k[at, :] += dot_nn(ds, q_t)
        dqt = dot_nn(kxt[:, pl.ds(base, SPAN * BLOCK)], dsb[0 : SPAN * BLOCK, :])
        dqt = dqt + dot_nn(kxt[:, EXT:], dsb[SPAN * BLOCK :, :])
        dq[pl.ds(base, TILE), :] = (dqt * SCALE).T.astype(BF16)
        return 0

    lax.fori_loop(0, OWN // TILE, tile, 0)
    dkv[0] = acc_k[HALO:EXT, :] * SCALE
    dkv[1] = acc_v[HALO:EXT, :]
    dh[0] = (acc_k[0:HALO, :] * SCALE).astype(BF16)
    dh[1] = acc_v[0:HALO, :].astype(BF16)
    ds_out[0] = (acc_k[EXT:, :] * SCALE).astype(BF16)
    ds_out[1] = acc_v[EXT:, :].astype(BF16)


def attn(sc, off, own, recv, halo, sums, base):
    width = own.shape[2]
    heads = width // HDIM
    keys = EXT + NSUM * BLOCK

    def by_head(n, rows):
        return pl.BlockSpec((n, rows, HDIM), lambda h, sc, off: (0, 0, h))

    sum_spec = pl.BlockSpec((2, BLOCK, HDIM), lambda h, sc, off: (0, 0, base + h))
    return pl.pallas_call(
        attn_kernel,
        grid_spec=pltpu.PrefetchScalarGridSpec(
            num_scalar_prefetch=2,
            grid=(heads,),
            in_specs=[by_head(4, OWN // 2), by_head(4, OWN // 2), by_head(2, HALO)]
            + [sum_spec] * NSUM,
            out_specs=[
                pl.BlockSpec((OWN, HDIM), lambda h, sc, off: (0, h)),
                by_head(2, OWN),
                by_head(2, HALO),
                by_head(2, NSUM * BLOCK),
            ],
            scratch_shapes=[
                pltpu.VMEM((keys, HDIM), BF16),
                pltpu.VMEM((keys, HDIM), BF16),
                pltpu.VMEM((OWN, HDIM), BF16),
                pltpu.VMEM((OWN, HDIM), BF16),
                pltpu.VMEM((HDIM, keys), BF16),
                pltpu.VMEM((keys, HDIM), F32),
                pltpu.VMEM((keys, HDIM), F32),
                pltpu.VMEM((ROWS, TILE), F32),
                pltpu.VMEM((ROWS, TILE), F32),
                pltpu.VMEM((ROWS, TILE), BF16),
            ],
        ),
        out_shape=[
            jax.ShapeDtypeStruct((OWN, width), BF16),
            jax.ShapeDtypeStruct((2, OWN, width), F32),
            jax.ShapeDtypeStruct((2, HALO, width), BF16),
            jax.ShapeDtypeStruct((2, NSUM * BLOCK, width), BF16),
        ],
        compiler_params=params(),
        cost_estimate=cost(heads * 96 * 10 * 128**3 * 2, heads * 4_000_000),
        name="attn",
    )(sc, off, own, recv, halo, *sums)


def finish_kernel(sc, off, dq, dkv, back, *refs):
    tots, outs = refs[:SIDE], refs[SIDE:]
    core, y, z, x = sc[1], sc[2], sc[3], sc[4]
    local = off[y] & 7
    here = (off[y] >> 3) == z
    total = tots[0][...].astype(F32)
    for part in tots[1:]:
        total = total + part[...].astype(F32)
    for step in range(SIDE):
        for side in range(2):
            block = ((core + side) & 1) * SIDE + ((x + step) & 3)
            rows = pl.ds(pl.multiple_of(block * BLOCK, BLOCK), BLOCK)
            prior = pl.multiple_of(jnp.maximum(block - 1, 0) * BLOCK, BLOCK)
            value = dkv[:, rows, :]
            value = value + jnp.where(block > 0, back[:, pl.ds(prior, BLOCK), :].astype(F32), 0.0)
            value = value + jnp.where(here & (local == block), total, 0.0)
            outs[step][side, 0] = dq[rows, :]
            outs[step][side, 1:3] = value.astype(BF16)


def finish(sc, off, dq, dkv, back, tots, base):
    width = dq.shape[1]
    shape = (2, 3, BLOCK, width)
    return pl.pallas_call(
        finish_kernel,
        grid_spec=pltpu.PrefetchScalarGridSpec(
            num_scalar_prefetch=2,
            grid=(width // HDIM,),
            in_specs=[
                pl.BlockSpec((OWN, HDIM), lambda h, sc, off: (0, h)),
                pl.BlockSpec((2, OWN, HDIM), lambda h, sc, off: (0, 0, h)),
                pl.BlockSpec((2, HALO, HDIM), lambda h, sc, off: (0, 0, h)),
            ]
            + [pl.BlockSpec((2, BLOCK, HDIM), lambda h, sc, off: (0, 0, base + h))] * SIDE,
            out_specs=[pl.BlockSpec((2, 3, BLOCK, HDIM), lambda h, sc, off: (0, 0, 0, h))] * SIDE,
        ),
        out_shape=[jax.ShapeDtypeStruct(shape, BF16)] * SIDE,
        compiler_params=params(),
        cost_estimate=cost(0, 20 * OWN * width),
        name="finish",
    )(sc, off, dq, dkv, back, *tots)


def place_kernel(sc, off, *refs):
    groups = len(SIZES)
    outs = refs[2 * SIDE * groups :]
    x, core = sc[4], sc[1]
    heads = sum(SIZES)
    at = 0
    for g in range(groups):
        width = SIZES[g] * HDIM
        for step in range(SIDE):
            source = (x + SIDE - step) & 3
            for part in range(2):
                side = core if part == 0 else 1 - core
                first = pl.multiple_of(((source * 2 + side) * heads + at) * HDIM, HDIM)
                ref = refs[(g * SIDE + step) * 2 + part]
                for n in range(3):
                    outs[n][:, pl.ds(first, width)] = ref[0, n]
        at += SIZES[g]


def place(sc, off, parts):
    columns = sum(SIZES) * HDIM * 2 * SIDE
    shape = (BLOCK, columns)
    specs = [pl.BlockSpec((1, *p.shape[1:]), lambda i, sc, off: (0, 0, 0, 0)) for p in parts]
    return pl.pallas_call(
        place_kernel,
        grid_spec=pltpu.PrefetchScalarGridSpec(
            num_scalar_prefetch=2,
            grid=(1,),
            in_specs=specs,
            out_specs=[whole(shape)] * 3,
        ),
        out_shape=[jax.ShapeDtypeStruct(shape, BF16)] * 3,
        compiler_params=params(),
        cost_estimate=cost(0, 12 * BLOCK * columns),
        name="place",
    )(sc, off, *parts)


def named(value, pairs, axis="ctx"):
    return lax.ppermute(value, axis, pairs)


def on_device(query, key_in, value_in, dout, off):
    width = query.shape[1]
    me = lax.axis_index("ctx")
    x = lax.axis_index("tp")
    which = lax.iota(jnp.int32, 8)
    sc = jnp.where(which == 0, me >> 1, me & 1)
    sc = jnp.where(which == 2, me >> 3, sc)
    sc = jnp.where(which == 3, (me >> 1) & 3, sc)
    sc = jnp.where(which == 4, x, sc).astype(jnp.int32)
    y, z = me >> 3, (me >> 1) & 3

    own_cand, oth_cand = candidate(sc, off, key_in, value_in)
    pieces = pieces_of(sc, off, own_cand, named(oth_cand, SWAP))
    arrived = [pieces[0]]
    arrived += [named(pieces[n], along_z(n)) for n in range(1, SIDE)]
    step = (z - (off[y] >> 3)) & 3
    piece = arrived[0]
    for n in range(1, SIDE):
        piece = jnp.where(step == n, arrived[n], piece)
    parts = [piece] + [named(piece, along_z(n)) for n in range(1, SIDE)]
    summary = gather(sc, off, parts)
    sums = [summary] + [named(summary, along_y(n)) for n in range(1, SIDE)]

    bases = [sum(SIZES[:g]) for g in range(len(SIZES))]
    owns, recvs, halos = [], [], []
    for g, heads in enumerate(SIZES):
        own, oth = pack(sc, off, (query, dout, key_in, value_in), bases[g], heads, width)
        recv = named(oth, SWAP)
        owns.append(own)
        recvs.append(recv)
        halos.append(named(halo_of(sc, off, own, recv), ring(1)))

    results = [None] * len(SIZES)
    for batch in BATCHES:
        done = []
        for g in batch:
            dq, dkv, dh, dsum = attn(sc, off, owns[g], recvs[g], halos[g], sums, bases[g])
            done.append((dq, dkv, named(dh, ring(-1)), dsum))
        sent = jnp.concatenate([d[3] for d in done], axis=2) if len(done) > 1 else done[0][3]
        part = sent[:, :BLOCK].astype(F32)
        for n in range(1, NSUM):
            moved = named(sent[:, n * BLOCK : (n + 1) * BLOCK], along_y(-n))
            part = part + moved.astype(F32)
        part = part.astype(BF16)
        tots = [part] + [named(part, along_z(n)) for n in range(1, SIDE)]
        for i, g in enumerate(batch):
            dq, dkv, back, _ = done[i]
            cuts = finish(sc, off, dq, dkv, back, tots, bases[g] - bases[batch[0]])
            there = [cuts[0]]
            there += [named(cuts[n], along_x(n), "tp") for n in range(1, SIDE)]
            both = []
            for n in range(SIDE):
                both += [there[n], named(there[n][1:], SWAP)]
            results[g] = both
    return tuple(place(sc, off, [p for both in results for p in both]))


def solution(mesh):
    return jax.shard_map(
        on_device,
        mesh=mesh,
        in_specs=(P("ctx", "tp"), P("ctx", "tp"), P("ctx", "tp"), P("ctx", "tp"), P()),
        out_specs=(P(("ctx", "tp"), None),) * 3,
        check_vma=False,
    )
```

```python
import functools
import math

import jax
import jax.numpy as jnp
from jax import lax
from jax.experimental import pallas as pl
from jax.experimental.pallas import tpu as pltpu
from jax.sharding import PartitionSpec as P


HDIM = 128
BLOCK = 128
BAND = 8
STRIDE = 32
CHIP_BLOCKS = 8
HALO = (BAND - 1) * BLOCK
OWN = CHIP_BLOCKS * BLOCK
EXT = HALO + OWN
TILE = 256
NSUM = 4
SPAN = 9
ROWS = (SPAN + NSUM) * BLOCK
NEG = -1e30
SIZES = (2, 2, 2)
CHIPS = 16
SIDE = 4
SCALE = HDIM**-0.5
LOG2E = math.log2(math.e)
BF16 = jnp.bfloat16
F32 = jnp.float32


def ring(step):
    return [(2 * c + k, 2 * ((c + step) % CHIPS) + k) for c in range(CHIPS) for k in range(2)]


def along_z(step):
    return [
        (2 * (y * SIDE + z) + k, 2 * (y * SIDE + (z + step) % SIDE) + k)
        for y in range(SIDE)
        for z in range(SIDE)
        for k in range(2)
    ]


def along_y(step):
    return [
        (2 * (y * SIDE + z) + k, 2 * ((y + step) % SIDE * SIDE + z) + k)
        for y in range(SIDE)
        for z in range(SIDE)
        for k in range(2)
    ]


SWAP = [(d, d ^ 1) for d in range(2 * CHIPS)]


def along_x(step):
    return [(x, (x + step) % SIDE) for x in range(SIDE)]


def params(**kw):
    return pltpu.CompilerParams(vmem_limit_bytes=56 * 1024 * 1024, **kw)


def cost(flops, nbytes):
    return pl.CostEstimate(flops=flops, bytes_accessed=nbytes, transcendentals=0)


def whole(shape):
    return pl.BlockSpec(shape, lambda *_: (0,) * len(shape))


def pack_kernel(sc, off, *refs):
    ins, (own, oth) = refs[:8], refs[8:]
    for n in range(4):
        own[n] = ins[2 * n][...]
        oth[n] = ins[2 * n + 1][...]


def pack(sc, off, arrays, base, heads, width):
    rows = arrays[0].shape[0]
    half = width // HDIM // 2
    chunk = 256
    cols = heads * HDIM
    specs, args = [], []
    for array in arrays:
        for other in (0, 1):
            specs.append(
                pl.BlockSpec(
                    (chunk, cols),
                    lambda i, sc, off, other=other: (
                        i,
                        jnp.abs(sc[1] - other) * (half // heads) + base // heads,
                    ),
                )
            )
            args.append(array)
    out = pl.BlockSpec((4, chunk, cols), lambda i, sc, off: (0, i, 0))
    shape = jax.ShapeDtypeStruct((4, rows, cols), BF16)
    return pl.pallas_call(
        pack_kernel,
        grid_spec=pltpu.PrefetchScalarGridSpec(
            num_scalar_prefetch=2,
            grid=(rows // chunk,),
            in_specs=specs,
            out_specs=[out, out],
        ),
        out_shape=[shape, shape],
        compiler_params=params(),
        cost_estimate=cost(0, 16 * rows * cols * 2),
        name="pack",
    )(sc, off, *args)


def halo_kernel(skip, sc, off, own, recv, out):
    lo = OWN // 2

    def fill(first, second):
        out[:, : lo - skip] = first[:, skip:]
        out[:, lo - skip :] = second[:, : lo - BLOCK + skip]

    pl.when(sc[1] == 0)(lambda: fill(own, recv))
    pl.when(sc[1] == 1)(lambda: fill(recv, own))


def halo_of(sc, off, own, recv, first):
    width = own.shape[2]
    spec = pl.BlockSpec((1, OWN // 2, width), lambda i, sc, off: (first + i, 0, 0))
    return pl.pallas_call(
        functools.partial(halo_kernel, BLOCK if first else 0),
        grid_spec=pltpu.PrefetchScalarGridSpec(
            num_scalar_prefetch=2,
            grid=(2,),
            in_specs=[spec, spec],
            out_specs=pl.BlockSpec((1, HALO, width), lambda i, sc, off: (i, 0, 0)),
        ),
        out_shape=jax.ShapeDtypeStruct((2, HALO, width), BF16),
        compiler_params=params(),
        cost_estimate=cost(0, 8 * OWN * width * 2),
        name="halo",
    )(sc, off, own, recv)


def candidate_kernel(sc, off, key, value, own, oth):
    half = own.shape[2]
    for n, ref in enumerate((key, value)):
        own[n] = ref[:, pl.ds(pl.multiple_of(sc[1] * half, HDIM), half)]
        oth[n] = ref[:, pl.ds(pl.multiple_of((1 - sc[1]) * half, HDIM), half)]


def candidate(sc, off, key, value):
    width = key.shape[1]
    spec = pl.BlockSpec((BLOCK, width), lambda i, sc, off: (off[sc[2]] & 3, 0))
    shape = (2, BLOCK, width // 2)
    return pl.pallas_call(
        candidate_kernel,
        grid_spec=pltpu.PrefetchScalarGridSpec(
            num_scalar_prefetch=2, grid=(1,), in_specs=[spec] * 2, out_specs=[whole(shape)] * 2
        ),
        out_shape=[jax.ShapeDtypeStruct(shape, BF16)] * 2,
        compiler_params=params(),
        cost_estimate=cost(0, 8 * BLOCK * width),
        name="candidate",
    )(sc, off, key, value)


def pieces_kernel(sc, off, own, recv, *outs):
    piece = BLOCK // SIDE
    mine = ((off[sc[2]] & 7) >> 2) == sc[1]
    for step in range(SIDE):
        row = pl.multiple_of(((sc[3] + step) & 3) * piece, piece)

        def put(ref, out=outs[step], row=row):
            out[...] = ref[:, pl.ds(row, piece), :]

        pl.when(mine)(functools.partial(put, own))
        pl.when(jnp.logical_not(mine))(functools.partial(put, recv))


def pieces_of(sc, off, own, recv):
    shape = (2, BLOCK // SIDE, own.shape[2])
    return pl.pallas_call(
        pieces_kernel,
        grid_spec=pltpu.PrefetchScalarGridSpec(
            num_scalar_prefetch=2,
            grid=(1,),
            in_specs=[whole(own.shape)] * 2,
            out_specs=[whole(shape)] * SIDE,
        ),
        out_shape=[jax.ShapeDtypeStruct(shape, BF16)] * SIDE,
        compiler_params=params(),
        cost_estimate=cost(0, 8 * own.size),
        name="pieces",
    )(sc, off, own, recv)


def gather_kernel(sc, off, *refs):
    out = refs[SIDE]
    piece = BLOCK // SIDE
    for step in range(SIDE):
        row = pl.multiple_of(((sc[3] + SIDE - step) % SIDE) * piece, piece)
        out[:, pl.ds(row, piece), :] = refs[step][...]


def gather(sc, off, pieces):
    shape = pieces[0].shape
    full = (2, BLOCK, shape[2])
    return pl.pallas_call(
        gather_kernel,
        grid_spec=pltpu.PrefetchScalarGridSpec(
            num_scalar_prefetch=2, grid=(1,), in_specs=[whole(shape)] * SIDE, out_specs=whole(full)
        ),
        out_shape=jax.ShapeDtypeStruct(full, BF16),
        compiler_params=params(),
        cost_estimate=cost(0, 4 * BLOCK * shape[2] * 2),
        name="gather",
    )(sc, off, *pieces)


def fold(x, op):
    return op(x.reshape(x.shape[0] // 8, 8, x.shape[1]), axis=0)


def spread(x):
    return x.reshape(x.shape[0] // 8, 8, x.shape[1])


def dot_nt(a, b):
    return lax.dot_general(a, b, (((1,), (1,)), ((), ())), preferred_element_type=F32)


def dot_nn(a, b):
    return lax.dot_general(a, b, (((1,), (0,)), ((), ())), preferred_element_type=F32)


def load_own(buf, own, recv, core, n, start):
    half = OWN // 2
    buf[pl.ds(pl.multiple_of(start + core * half, BLOCK), half), :] = own[n]
    buf[pl.ds(pl.multiple_of(start + (1 - core) * half, BLOCK), half), :] = recv[n]


def attn_kernel(sc, off, own, recv, halo, s0, s1, s2, s3, dq, dkv, stat, ds_out, *scratch):
    kx, vx, qs, dos, kxt, acc_k, acc_v, xs, dps, dsb = scratch
    core, chip, y = sc[1], sc[0], sc[2]
    load_own(qs, own, recv, core, 0, 0)
    load_own(dos, own, recv, core, 1, 0)
    for buf, n in ((kx, 0), (vx, 1)):
        buf[0:HALO, :] = halo[n]
        load_own(buf, own, recv, core, 2 + n, HALO)
        for s, part in enumerate((s0, s1, s2, s3)):
            buf[EXT + s * BLOCK : EXT + (s + 1) * BLOCK, :] = part[n]
    kxt[...] = kx[...].T
    acc_k[...] = jnp.zeros_like(acc_k)
    acc_v[...] = jnp.zeros_like(acc_v)
    row = lax.broadcasted_iota(jnp.int32, (BLOCK, TILE), 0)
    col = lax.broadcasted_iota(jnp.int32, (BLOCK, TILE), 1)
    first = lax.broadcasted_iota(jnp.int32, (1, TILE), 1) < BLOCK
    outside = jnp.where(chip == 0, NEG, 0.0)

    for t in range(OWN // TILE):
        base = t * TILE
        q_t = qs[base : base + TILE, :]
        do_t = dos[base : base + TILE, :]

        def start_of(j, base=base):
            return base + j * BLOCK if j < SPAN else EXT + (j - SPAN) * BLOCK

        m8 = jnp.full((8, TILE), NEG, F32)
        l8 = jnp.zeros((8, TILE), F32)
        d8 = jnp.zeros((8, TILE), F32)
        tops = []
        for j in range(SPAN + NSUM):
            span = slice(j * BLOCK, (j + 1) * BLOCK)
            at = slice(start_of(j), start_of(j) + BLOCK)
            x = dot_nt(kx[at, :], q_t) * (SCALE * LOG2E)
            if start_of(j) < HALO:
                x = x + outside
            if j == 0:
                x = jnp.where(first, x, NEG)
            if j == BAND - 1:
                x = jnp.where(row <= col, x, NEG)
            if j == BAND:
                x = jnp.where(row + BLOCK <= col, x, NEG)
            if j >= SPAN:
                slot = (y + NSUM - (j - SPAN)) & 3
                g = slot * STRIDE + off[slot]
                block = chip * CHIP_BLOCKS + 2 * t - (BAND - 1)
                b0 = jnp.where(g < block, 0.0, NEG)
                b1 = jnp.where(g < block + 1, 0.0, NEG)
                x = x + jnp.where(first, b0, b1)
            dp = dot_nt(vx[at, :], do_t)
            top = jnp.maximum(m8, fold(x, jnp.max))
            fade = jnp.exp2(m8 - top)
            p = jnp.exp2(spread(x) - top[None])
            l8 = l8 * fade + jnp.sum(p, axis=0)
            d8 = d8 * fade + jnp.sum(p * spread(dp), axis=0)
            xs[span, :] = p.reshape(BLOCK, TILE)
            dps[span, :] = dp
            m8 = top
            tops.append(top)
        m = jnp.max(m8, axis=0, keepdims=True)
        rest = jnp.exp2(m8 - m)
        total = jnp.sum(l8 * rest, axis=0, keepdims=True)
        inv = 1.0 / total
        delta = jnp.sum(d8 * rest, axis=0, keepdims=True) * inv
        stat[0, 0:1, base : base + TILE] = m + jnp.log2(total)
        stat[0, 1:2, base : base + TILE] = delta
        for j in range(SPAN + NSUM):
            span = slice(j * BLOCK, (j + 1) * BLOCK)
            factor = jnp.exp2(tops[j] - m) * inv
            p = (spread(xs[span, :]) * factor[None]).reshape(BLOCK, TILE)
            ds = (p * (dps[span, :] - delta)).astype(BF16)
            dsb[span, :] = ds
            if start_of(j) >= HALO:
                to = slice(start_of(j) - HALO, start_of(j) - HALO + BLOCK)
                acc_v[to, :] += dot_nn(p.astype(BF16), do_t)
                acc_k[to, :] += dot_nn(ds, q_t)
        dqt = dot_nn(kxt[:, base : base + SPAN * BLOCK], dsb[0 : SPAN * BLOCK, :])
        dqt = dqt + dot_nn(kxt[:, EXT:], dsb[SPAN * BLOCK :, :])
        dq[base : base + TILE, :] = (dqt * SCALE).T.astype(BF16)

    dkv[0] = acc_k[0:OWN, :]
    dkv[1] = acc_v[0:OWN, :]
    ds_out[0] = (acc_k[OWN:, :] * SCALE).astype(BF16)
    ds_out[1] = acc_v[OWN:, :].astype(BF16)


def later_kernel(sc, off, own, recv, qd, stat, dkv, out, kx, vx, qs, dos, acc_k, acc_v):
    core, chip = sc[1], sc[0]
    load_own(kx, own, recv, core, 0, 0)
    load_own(vx, own, recv, core, 1, 0)
    for buf, n in ((qs, 0), (dos, 1)):
        buf[0:HALO, :] = qd[n]
        buf[HALO:, :] = jnp.zeros((OWN - HALO, HDIM), BF16)
    acc_k[...] = dkv[0]
    acc_v[...] = dkv[1]
    first = lax.broadcasted_iota(jnp.int32, (1, TILE), 1) < BLOCK
    outside = jnp.where(chip == CHIPS - 1, NEG, 0.0)
    for t in range(OWN // TILE):
        base = t * TILE
        q_t = qs[base : base + TILE, :]
        do_t = dos[base : base + TILE, :]
        shift = outside - stat[0, 0:1, base : base + TILE]
        delta = stat[0, 1:2, base : base + TILE]
        for j in range(2 * t + 1, CHIP_BLOCKS):
            at = slice(j * BLOCK, (j + 1) * BLOCK)
            x = dot_nt(kx[at, :], q_t) * (SCALE * LOG2E) + shift
            if j == 2 * t + 1:
                x = jnp.where(first, x, NEG)
            p = jnp.exp2(x)
            ds = (p * (dot_nt(vx[at, :], do_t) - delta)).astype(BF16)
            acc_v[at, :] += dot_nn(p.astype(BF16), do_t)
            acc_k[at, :] += dot_nn(ds, q_t)
    out[0] = acc_k[...] * SCALE
    out[1] = acc_v[...]


def later(sc, off, own, recv, qd, stat, dkv):
    width = own.shape[2]
    heads = width // HDIM
    pair = pl.BlockSpec((2, OWN // 2, HDIM), lambda h, sc, off: (1, 0, h))
    full = pl.BlockSpec((2, OWN, HDIM), lambda h, sc, off: (0, 0, h))
    return pl.pallas_call(
        later_kernel,
        grid_spec=pltpu.PrefetchScalarGridSpec(
            num_scalar_prefetch=2,
            grid=(heads,),
            in_specs=[
                pair,
                pair,
                pl.BlockSpec((2, HALO, HDIM), lambda h, sc, off: (0, 0, h)),
                pl.BlockSpec((1, 8, OWN), lambda h, sc, off: (h, 0, 0)),
                full,
            ],
            out_specs=full,
            scratch_shapes=[pltpu.VMEM((OWN, HDIM), BF16)] * 4
            + [pltpu.VMEM((OWN, HDIM), F32)] * 2,
        ),
        out_shape=jax.ShapeDtypeStruct((2, OWN, width), F32),
        compiler_params=params(),
        cost_estimate=cost(heads * 28 * 8 * 128**3 * 2, heads * 4_000_000),
        name="later",
    )(sc, off, own, recv, qd, stat, dkv)


def attn(sc, off, own, recv, halo, sums):
    width = own.shape[2]
    heads = width // HDIM
    keys = EXT + NSUM * BLOCK

    def by_head(n, rows):
        return pl.BlockSpec((n, rows, HDIM), lambda h, sc, off: (0, 0, h))

    sum_spec = pl.BlockSpec((2, BLOCK, HDIM), lambda h, sc, off: (0, 0, h))
    return pl.pallas_call(
        attn_kernel,
        grid_spec=pltpu.PrefetchScalarGridSpec(
            num_scalar_prefetch=2,
            grid=(heads,),
            in_specs=[by_head(4, OWN // 2), by_head(4, OWN // 2), by_head(2, HALO)]
            + [sum_spec] * NSUM,
            out_specs=[
                pl.BlockSpec((OWN, HDIM), lambda h, sc, off: (0, h)),
                by_head(2, OWN),
                pl.BlockSpec((1, 8, OWN), lambda h, sc, off: (h, 0, 0)),
                by_head(2, NSUM * BLOCK),
            ],
            scratch_shapes=[
                pltpu.VMEM((keys, HDIM), BF16),
                pltpu.VMEM((keys, HDIM), BF16),
                pltpu.VMEM((OWN, HDIM), BF16),
                pltpu.VMEM((OWN, HDIM), BF16),
                pltpu.VMEM((HDIM, keys), BF16),
                pltpu.VMEM((OWN + NSUM * BLOCK, HDIM), F32),
                pltpu.VMEM((OWN + NSUM * BLOCK, HDIM), F32),
                pltpu.VMEM((ROWS, TILE), F32),
                pltpu.VMEM((ROWS, TILE), F32),
                pltpu.VMEM((ROWS, TILE), BF16),
            ],
        ),
        out_shape=[
            jax.ShapeDtypeStruct((OWN, width), BF16),
            jax.ShapeDtypeStruct((2, OWN, width), F32),
            jax.ShapeDtypeStruct((heads, 8, OWN), F32),
            jax.ShapeDtypeStruct((2, NSUM * BLOCK, width), BF16),
        ],
        compiler_params=params(),
        cost_estimate=cost(heads * 96 * 10 * 128**3 * 2, heads * 4_000_000),
        name="attn",
    )(sc, off, own, recv, halo, *sums)


def finish_kernel(sc, off, dq, dkv, *refs):
    tots, outs = refs[:SIDE], refs[SIDE:]
    core, y, z, x = sc[1], sc[2], sc[3], sc[4]
    local = off[y] & 7
    here = (off[y] >> 3) == z
    total = tots[0][...].astype(F32)
    for part in tots[1:]:
        total = total + part[...].astype(F32)
    for step in range(SIDE):
        for side in range(2):
            block = ((core + side) & 1) * SIDE + ((x + step) & 3)
            rows = pl.ds(pl.multiple_of(block * BLOCK, BLOCK), BLOCK)
            value = dkv[:, rows, :] + jnp.where(here & (local == block), total, 0.0)
            outs[step][side, 0] = dq[rows, :]
            outs[step][side, 1:3] = value.astype(BF16)


def finish(sc, off, dq, dkv, tots):
    width = dq.shape[1]
    shape = (2, 3, BLOCK, width)
    return pl.pallas_call(
        finish_kernel,
        grid_spec=pltpu.PrefetchScalarGridSpec(
            num_scalar_prefetch=2,
            grid=(width // HDIM,),
            in_specs=[
                pl.BlockSpec((OWN, HDIM), lambda h, sc, off: (0, h)),
                pl.BlockSpec((2, OWN, HDIM), lambda h, sc, off: (0, 0, h)),
            ]
            + [pl.BlockSpec((2, BLOCK, HDIM), lambda h, sc, off: (0, 0, h))] * SIDE,
            out_specs=[pl.BlockSpec((2, 3, BLOCK, HDIM), lambda h, sc, off: (0, 0, 0, h))] * SIDE,
        ),
        out_shape=[jax.ShapeDtypeStruct(shape, BF16)] * SIDE,
        compiler_params=params(),
        cost_estimate=cost(0, 20 * OWN * width),
        name="finish",
    )(sc, off, dq, dkv, *tots)


def place_kernel(sc, off, *refs):
    groups = len(SIZES)
    outs = refs[(SIDE + 1) * groups :]
    x, core = sc[4], sc[1]
    heads = sum(SIZES)
    at = 0
    for g in range(groups):
        width = SIZES[g] * HDIM
        for step in range(SIDE):
            source = (x + SIDE - step) & 3
            for part in range(2):
                side = core if part == 0 else 1 - core
                first = pl.multiple_of(((source * 2 + side) * heads + at) * HDIM, HDIM)
                ref = refs[g * (SIDE + 1) + (step if part == 0 else SIDE)]
                for n in range(3):
                    outs[n][:, pl.ds(first, width)] = ref[0 if part == 0 else step, n]
        at += SIZES[g]


def place(sc, off, parts):
    columns = sum(SIZES) * HDIM * 2 * SIDE
    shape = (BLOCK, columns)
    specs = []
    for n, p in enumerate(parts):
        lead = SIDE if n % (SIDE + 1) == SIDE else 1
        specs.append(pl.BlockSpec((lead, *p.shape[1:]), lambda i, sc, off: (0, 0, 0, 0)))
    return pl.pallas_call(
        place_kernel,
        grid_spec=pltpu.PrefetchScalarGridSpec(
            num_scalar_prefetch=2,
            grid=(1,),
            in_specs=specs,
            out_specs=[whole(shape)] * 3,
        ),
        out_shape=[jax.ShapeDtypeStruct(shape, BF16)] * 3,
        compiler_params=params(),
        cost_estimate=cost(0, 12 * BLOCK * columns),
        name="place",
    )(sc, off, *parts)


def named(value, pairs, axis="ctx"):
    return lax.ppermute(value, axis, pairs)


def on_device(query, key_in, value_in, dout, off):
    width = query.shape[1]
    me = lax.axis_index("ctx")
    x = lax.axis_index("tp")
    which = lax.iota(jnp.int32, 8)
    sc = jnp.where(which == 0, me >> 1, me & 1)
    sc = jnp.where(which == 2, me >> 3, sc)
    sc = jnp.where(which == 3, (me >> 1) & 3, sc)
    sc = jnp.where(which == 4, x, sc).astype(jnp.int32)
    y, z = me >> 3, (me >> 1) & 3

    own_cand, oth_cand = candidate(sc, off, key_in, value_in)
    pieces = pieces_of(sc, off, own_cand, named(oth_cand, SWAP))
    arrived = [pieces[0]]
    arrived += [named(pieces[n], along_z(n)) for n in range(1, SIDE)]
    step = (z - (off[y] >> 3)) & 3
    piece = arrived[0]
    for n in range(1, SIDE):
        piece = jnp.where(step == n, arrived[n], piece)
    parts = [piece] + [named(piece, along_z(n)) for n in range(1, SIDE)]
    summary = gather(sc, off, parts)

    bases = [sum(SIZES[:g]) for g in range(len(SIZES))]
    work = []
    for g, heads in enumerate(SIZES):
        own, oth = pack(sc, off, (query, dout, key_in, value_in), bases[g], heads, width)
        recv = named(oth, SWAP)
        kv = named(halo_of(sc, off, own, recv, 2), ring(1))
        qd = named(halo_of(sc, off, own, recv, 0), ring(-1))
        work.append((own, recv, kv, qd))

    parts = []
    for g, heads in enumerate(SIZES):
        own, recv, kv, qd = work[g]
        mine = summary[:, :, bases[g] * HDIM : (bases[g] + heads) * HDIM]
        sums = [mine] + [named(mine, along_y(n)) for n in range(1, NSUM)]
        dq, dkv, stat, sent = attn(sc, off, own, recv, kv, sums)
        stat = named(stat, ring(-1))
        dkv = later(sc, off, own, recv, qd, stat, dkv)
        part = sent[:, :BLOCK].astype(F32)
        for n in range(1, NSUM):
            moved = named(sent[:, n * BLOCK : (n + 1) * BLOCK], along_y(-n))
            part = part + moved.astype(F32)
        part = part.astype(BF16)
        tots = [part] + [named(part, along_z(n)) for n in range(1, SIDE)]
        cuts = finish(sc, off, dq, dkv, tots)
        there = [cuts[0]]
        there += [named(cuts[n], along_x(n), "tp") for n in range(1, SIDE)]
        parts += there
        parts.append(named(jnp.concatenate([t[1:] for t in there], axis=0), SWAP))
    return tuple(place(sc, off, parts))


def solution(mesh):
    return jax.shard_map(
        on_device,
        mesh=mesh,
        in_specs=(P("ctx", "tp"), P("ctx", "tp"), P("ctx", "tp"), P("ctx", "tp"), P()),
        out_specs=(P(("ctx", "tp"), None),) * 3,
        check_vma=False,
    )
```

```python
import functools
import math

import jax
import jax.numpy as jnp
from jax import lax
from jax.experimental import pallas as pl
from jax.experimental.pallas import tpu as pltpu
from jax.sharding import PartitionSpec as P


HDIM = 128
BLOCK = 128
BAND = 8
STRIDE = 32
CHIP_BLOCKS = 8
HALO = (BAND - 1) * BLOCK
OWN = CHIP_BLOCKS * BLOCK
EXT = HALO + OWN
TILE = 256
NSUM = 4
SPAN = 9
ROWS = (SPAN + NSUM) * BLOCK
NEG = -1e30
SIZES = (3, 3)
CHIPS = 16
SIDE = 4
SCALE = HDIM**-0.5
LOG2E = math.log2(math.e)
BF16 = jnp.bfloat16
F32 = jnp.float32


def ring(step):
    return [(2 * c + k, 2 * ((c + step) % CHIPS) + k) for c in range(CHIPS) for k in range(2)]


def along_z(step):
    return [
        (2 * (y * SIDE + z) + k, 2 * (y * SIDE + (z + step) % SIDE) + k)
        for y in range(SIDE)
        for z in range(SIDE)
        for k in range(2)
    ]


def along_y(step):
    return [
        (2 * (y * SIDE + z) + k, 2 * ((y + step) % SIDE * SIDE + z) + k)
        for y in range(SIDE)
        for z in range(SIDE)
        for k in range(2)
    ]


SWAP = [(d, d ^ 1) for d in range(2 * CHIPS)]


def along_x(step):
    return [(x, (x + step) % SIDE) for x in range(SIDE)]


def params(**kw):
    return pltpu.CompilerParams(vmem_limit_bytes=56 * 1024 * 1024, **kw)


def cost(flops, nbytes):
    return pl.CostEstimate(flops=flops, bytes_accessed=nbytes, transcendentals=0)


def whole(shape):
    return pl.BlockSpec(shape, lambda *_: (0,) * len(shape))


def pack_kernel(sc, off, *refs):
    ins, (own, oth) = refs[:8], refs[8:]
    for n in range(4):
        own[n] = ins[2 * n][...]
        oth[n] = ins[2 * n + 1][...]


def pack(sc, off, arrays, base, heads, width):
    rows = arrays[0].shape[0]
    half = width // HDIM // 2
    chunk = 256
    cols = heads * HDIM
    specs, args = [], []
    for array in arrays:
        for other in (0, 1):
            specs.append(
                pl.BlockSpec(
                    (chunk, cols),
                    lambda i, sc, off, other=other: (
                        i,
                        jnp.abs(sc[1] - other) * (half // heads) + base // heads,
                    ),
                )
            )
            args.append(array)
    out = pl.BlockSpec((4, chunk, cols), lambda i, sc, off: (0, i, 0))
    shape = jax.ShapeDtypeStruct((4, rows, cols), BF16)
    return pl.pallas_call(
        pack_kernel,
        grid_spec=pltpu.PrefetchScalarGridSpec(
            num_scalar_prefetch=2,
            grid=(rows // chunk,),
            in_specs=specs,
            out_specs=[out, out],
        ),
        out_shape=[shape, shape],
        compiler_params=params(),
        cost_estimate=cost(0, 16 * rows * cols * 2),
        name="pack",
    )(sc, off, *args)


def halo_kernel(sc, off, own, recv, qd, kv):
    lo = OWN // 2

    def fill(first, second):
        @pl.when(pl.program_id(0) < 2)
        def _():
            qd[:, :lo] = first[...]
            qd[:, lo:] = second[:, : lo - BLOCK]

        @pl.when(pl.program_id(0) >= 2)
        def _():
            kv[:, : lo - BLOCK] = first[:, BLOCK:]
            kv[:, lo - BLOCK :] = second[...]

    pl.when(sc[1] == 0)(lambda: fill(own, recv))
    pl.when(sc[1] == 1)(lambda: fill(recv, own))


def halo_of(sc, off, own, recv):
    width = own.shape[2]
    spec = pl.BlockSpec((1, OWN // 2, width), lambda i, sc, off: (i, 0, 0))
    return pl.pallas_call(
        halo_kernel,
        grid_spec=pltpu.PrefetchScalarGridSpec(
            num_scalar_prefetch=2,
            grid=(4,),
            in_specs=[spec, spec],
            out_specs=[
                pl.BlockSpec((1, HALO, width), lambda i, sc, off: (jnp.minimum(i, 1), 0, 0)),
                pl.BlockSpec((1, HALO, width), lambda i, sc, off: (jnp.maximum(i - 2, 0), 0, 0)),
            ],
        ),
        out_shape=[jax.ShapeDtypeStruct((2, HALO, width), BF16)] * 2,
        compiler_params=params(),
        cost_estimate=cost(0, 16 * OWN * width * 2),
        name="halo",
    )(sc, off, own, recv)


def candidate_kernel(sc, off, key, value, own, oth):
    half = own.shape[2]
    for n, ref in enumerate((key, value)):
        own[n] = ref[:, pl.ds(pl.multiple_of(sc[1] * half, HDIM), half)]
        oth[n] = ref[:, pl.ds(pl.multiple_of((1 - sc[1]) * half, HDIM), half)]


def candidate(sc, off, key, value):
    width = key.shape[1]
    spec = pl.BlockSpec((BLOCK, width), lambda i, sc, off: (off[sc[2]] & 3, 0))
    shape = (2, BLOCK, width // 2)
    return pl.pallas_call(
        candidate_kernel,
        grid_spec=pltpu.PrefetchScalarGridSpec(
            num_scalar_prefetch=2, grid=(1,), in_specs=[spec] * 2, out_specs=[whole(shape)] * 2
        ),
        out_shape=[jax.ShapeDtypeStruct(shape, BF16)] * 2,
        compiler_params=params(),
        cost_estimate=cost(0, 8 * BLOCK * width),
        name="candidate",
    )(sc, off, key, value)


def pieces_kernel(sc, off, own, recv, *outs):
    piece = BLOCK // SIDE
    mine = ((off[sc[2]] & 7) >> 2) == sc[1]
    for step in range(SIDE):
        row = pl.multiple_of(((sc[3] + step) & 3) * piece, piece)

        def put(ref, out=outs[step], row=row):
            out[...] = ref[:, pl.ds(row, piece), :]

        pl.when(mine)(functools.partial(put, own))
        pl.when(jnp.logical_not(mine))(functools.partial(put, recv))


def pieces_of(sc, off, own, recv):
    shape = (2, BLOCK // SIDE, own.shape[2])
    return pl.pallas_call(
        pieces_kernel,
        grid_spec=pltpu.PrefetchScalarGridSpec(
            num_scalar_prefetch=2,
            grid=(1,),
            in_specs=[whole(own.shape)] * 2,
            out_specs=[whole(shape)] * SIDE,
        ),
        out_shape=[jax.ShapeDtypeStruct(shape, BF16)] * SIDE,
        compiler_params=params(),
        cost_estimate=cost(0, 8 * own.size),
        name="pieces",
    )(sc, off, own, recv)


def gather_kernel(sc, off, *refs):
    out = refs[SIDE]
    piece = BLOCK // SIDE
    for step in range(SIDE):
        row = pl.multiple_of(((sc[3] + SIDE - step) % SIDE) * piece, piece)
        out[:, pl.ds(row, piece), :] = refs[step][...]


def gather(sc, off, pieces):
    shape = pieces[0].shape
    full = (2, BLOCK, shape[2])
    return pl.pallas_call(
        gather_kernel,
        grid_spec=pltpu.PrefetchScalarGridSpec(
            num_scalar_prefetch=2, grid=(1,), in_specs=[whole(shape)] * SIDE, out_specs=whole(full)
        ),
        out_shape=jax.ShapeDtypeStruct(full, BF16),
        compiler_params=params(),
        cost_estimate=cost(0, 4 * BLOCK * shape[2] * 2),
        name="gather",
    )(sc, off, *pieces)


def fold(x, op):
    return op(x.reshape(x.shape[0] // 8, 8, x.shape[1]), axis=0)


def spread(x):
    return x.reshape(x.shape[0] // 8, 8, x.shape[1])


def dot_nt(a, b):
    return lax.dot_general(a, b, (((1,), (1,)), ((), ())), preferred_element_type=F32)


def dot_nn(a, b):
    return lax.dot_general(a, b, (((1,), (0,)), ((), ())), preferred_element_type=F32)


def load_own(buf, own, recv, core, n, start):
    half = OWN // 2
    buf[pl.ds(pl.multiple_of(start + core * half, BLOCK), half), :] = own[n]
    buf[pl.ds(pl.multiple_of(start + (1 - core) * half, BLOCK), half), :] = recv[n]


def attn_kernel(sc, off, own, recv, halo, s0, s1, s2, s3, dq, dkv, stat, ds_out, *scratch):
    kx, vx, qs, dos, kxt, xs, dps, dsb, pb = scratch
    core, chip, y = sc[1], sc[0], sc[2]
    load_own(qs, own, recv, core, 0, 0)
    load_own(dos, own, recv, core, 1, 0)
    for buf, n in ((kx, 0), (vx, 1)):
        buf[0:HALO, :] = halo[n]
        load_own(buf, own, recv, core, 2 + n, HALO)
        for s, part in enumerate((s0, s1, s2, s3)):
            buf[EXT + s * BLOCK : EXT + (s + 1) * BLOCK, :] = part[n]
    kxt[...] = kx[...].T
    row = lax.broadcasted_iota(jnp.int32, (BLOCK, TILE), 0)
    col = lax.broadcasted_iota(jnp.int32, (BLOCK, TILE), 1)
    first = lax.broadcasted_iota(jnp.int32, (1, TILE), 1) < BLOCK
    outside = jnp.where(chip == 0, NEG, 0.0)

    for t in range(OWN // TILE):
        base = t * TILE
        q_t = qs[base : base + TILE, :]
        do_t = dos[base : base + TILE, :]

        def start_of(j, base=base):
            return base + j * BLOCK if j < SPAN else EXT + (j - SPAN) * BLOCK

        m8 = jnp.full((8, TILE), NEG, F32)
        l8 = jnp.zeros((8, TILE), F32)
        d8 = jnp.zeros((8, TILE), F32)
        tops = []
        for j in range(SPAN + NSUM):
            span = slice(j * BLOCK, (j + 1) * BLOCK)
            at = slice(start_of(j), start_of(j) + BLOCK)
            x = dot_nt(kx[at, :], q_t) * (SCALE * LOG2E)
            if start_of(j) < HALO:
                x = x + outside
            if j == 0:
                x = jnp.where(first, x, NEG)
            if j == BAND - 1:
                x = jnp.where(row <= col, x, NEG)
            if j == BAND:
                x = jnp.where(row + BLOCK <= col, x, NEG)
            if j >= SPAN:
                slot = (y + NSUM - (j - SPAN)) & 3
                g = slot * STRIDE + off[slot]
                block = chip * CHIP_BLOCKS + 2 * t - (BAND - 1)
                b0 = jnp.where(g < block, 0.0, NEG)
                b1 = jnp.where(g < block + 1, 0.0, NEG)
                x = x + jnp.where(first, b0, b1)
            dp = dot_nt(vx[at, :], do_t)
            top = jnp.maximum(m8, fold(x, jnp.max))
            fade = jnp.exp2(m8 - top)
            p = jnp.exp2(spread(x) - top[None])
            l8 = l8 * fade + jnp.sum(p, axis=0)
            d8 = d8 * fade + jnp.sum(p * spread(dp), axis=0)
            xs[span, :] = p.reshape(BLOCK, TILE)
            dps[span, :] = dp
            m8 = top
            tops.append(top)
        m = jnp.max(m8, axis=0, keepdims=True)
        rest = jnp.exp2(m8 - m)
        total = jnp.sum(l8 * rest, axis=0, keepdims=True)
        inv = 1.0 / total
        delta = jnp.sum(d8 * rest, axis=0, keepdims=True) * inv
        stat[0, 0:1, base : base + TILE] = m + jnp.log2(total)
        stat[0, 1:2, base : base + TILE] = delta
        for j in range(SPAN + NSUM):
            span = slice(j * BLOCK, (j + 1) * BLOCK)
            factor = jnp.exp2(tops[j] - m) * inv
            p = (spread(xs[span, :]) * factor[None]).reshape(BLOCK, TILE)
            at = start_of(j)
            cols = slice(base, base + TILE)
            dsb[at : at + BLOCK, cols] = (p * (dps[span, :] - delta)).astype(BF16)
            if at >= HALO:
                pb[at - HALO : at - HALO + BLOCK, cols] = p.astype(BF16)
        cols = slice(base, base + TILE)
        dqt = dot_nn(kxt[:, base : base + SPAN * BLOCK], dsb[base : base + SPAN * BLOCK, cols])
        dqt = dqt + dot_nn(kxt[:, EXT:], dsb[EXT:, cols])
        dq[base : base + TILE, :] = (dqt * SCALE).T.astype(BF16)

    for t in range(OWN // TILE):
        keys = slice(t * TILE, (t + 1) * TILE)
        dkv[0, keys, :] = dot_nn(dsb[HALO + t * TILE : HALO + (t + 1) * TILE, t * TILE :], qs[t * TILE :, :])
        dkv[1, keys, :] = dot_nn(pb[keys, t * TILE :], dos[t * TILE :, :])
    for s in range(NSUM // 2):
        keys = slice(s * TILE, (s + 1) * TILE)
        ds_out[0, keys, :] = (
            dot_nn(dsb[EXT + s * TILE : EXT + (s + 1) * TILE, :], qs[...]) * SCALE
        ).astype(BF16)
        ds_out[1, keys, :] = dot_nn(pb[OWN + s * TILE : OWN + (s + 1) * TILE, :], dos[...]).astype(BF16)


def later_kernel(sc, off, own, recv, qd, stat, dkv, out, kx, vx, qs, dos, dsb, pb):
    core, chip = sc[1], sc[0]
    load_own(kx, own, recv, core, 0, 0)
    load_own(vx, own, recv, core, 1, 0)
    for buf, n in ((qs, 0), (dos, 1)):
        buf[0:HALO, :] = qd[n]
        buf[HALO:, :] = jnp.zeros((OWN - HALO, HDIM), BF16)
    first = lax.broadcasted_iota(jnp.int32, (1, TILE), 1) < BLOCK
    outside = jnp.where(chip == CHIPS - 1, NEG, 0.0)
    for t in range(OWN // TILE):
        cols = slice(t * TILE, (t + 1) * TILE)
        q_t = qs[cols, :]
        do_t = dos[cols, :]
        shift = outside - stat[0, 0:1, cols]
        delta = stat[0, 1:2, cols]
        for j in range(2 * t + 1, CHIP_BLOCKS):
            at = slice(j * BLOCK, (j + 1) * BLOCK)
            x = dot_nt(kx[at, :], q_t) * (SCALE * LOG2E) + shift
            if j == 2 * t + 1:
                x = jnp.where(first, x, NEG)
            p = jnp.exp2(x)
            dsb[at, cols] = (p * (dot_nt(vx[at, :], do_t) - delta)).astype(BF16)
            pb[at, cols] = p.astype(BF16)
    for j in range(0, CHIP_BLOCKS):
        at = slice(j * BLOCK, (j + 1) * BLOCK)
        upto = (j + 1) // 2 * TILE
        for n, (low, rows, by) in enumerate(((dsb, qs, SCALE), (pb, dos, 1.0))):
            value = dkv[n, at, :]
            if upto:
                value = value + dot_nn(low[at, :upto], rows[:upto, :])
            out[n, at, :] = value * by


def later(sc, off, own, recv, qd, stat, dkv):
    width = own.shape[2]
    heads = width // HDIM
    pair = pl.BlockSpec((2, OWN // 2, HDIM), lambda h, sc, off: (1, 0, h))
    full = pl.BlockSpec((2, OWN, HDIM), lambda h, sc, off: (0, 0, h))
    return pl.pallas_call(
        later_kernel,
        grid_spec=pltpu.PrefetchScalarGridSpec(
            num_scalar_prefetch=2,
            grid=(heads,),
            in_specs=[
                pair,
                pair,
                pl.BlockSpec((2, HALO, HDIM), lambda h, sc, off: (0, 0, h)),
                pl.BlockSpec((1, 8, OWN), lambda h, sc, off: (h, 0, 0)),
                full,
            ],
            out_specs=full,
            scratch_shapes=[pltpu.VMEM((OWN, HDIM), BF16)] * 4 + [pltpu.VMEM((OWN, OWN), BF16)] * 2,
        ),
        out_shape=jax.ShapeDtypeStruct((2, OWN, width), F32),
        compiler_params=params(),
        cost_estimate=cost(heads * 28 * 8 * 128**3 * 2, heads * 4_000_000),
        name="later",
    )(sc, off, own, recv, qd, stat, dkv)


def attn(sc, off, own, recv, halo, sums, base):
    width = own.shape[2]
    heads = width // HDIM
    keys = EXT + NSUM * BLOCK

    def by_head(n, rows):
        return pl.BlockSpec((n, rows, HDIM), lambda h, sc, off: (0, 0, h))

    sum_spec = pl.BlockSpec((2, BLOCK, HDIM), lambda h, sc, off: (0, 0, base + h))
    return pl.pallas_call(
        attn_kernel,
        grid_spec=pltpu.PrefetchScalarGridSpec(
            num_scalar_prefetch=2,
            grid=(heads,),
            in_specs=[by_head(4, OWN // 2), by_head(4, OWN // 2), by_head(2, HALO)]
            + [sum_spec] * NSUM,
            out_specs=[
                pl.BlockSpec((OWN, HDIM), lambda h, sc, off: (0, h)),
                by_head(2, OWN),
                pl.BlockSpec((1, 8, OWN), lambda h, sc, off: (h, 0, 0)),
                by_head(2, NSUM * BLOCK),
            ],
            scratch_shapes=[
                pltpu.VMEM((keys, HDIM), BF16),
                pltpu.VMEM((keys, HDIM), BF16),
                pltpu.VMEM((OWN, HDIM), BF16),
                pltpu.VMEM((OWN, HDIM), BF16),
                pltpu.VMEM((HDIM, keys), BF16),
                pltpu.VMEM((ROWS, TILE), F32),
                pltpu.VMEM((ROWS, TILE), F32),
                pltpu.VMEM((keys, OWN), BF16),
                pltpu.VMEM((OWN + NSUM * BLOCK, OWN), BF16),
            ],
        ),
        out_shape=[
            jax.ShapeDtypeStruct((OWN, width), BF16),
            jax.ShapeDtypeStruct((2, OWN, width), F32),
            jax.ShapeDtypeStruct((heads, 8, OWN), F32),
            jax.ShapeDtypeStruct((2, NSUM * BLOCK, width), BF16),
        ],
        compiler_params=params(),
        cost_estimate=cost(heads * 96 * 10 * 128**3 * 2, heads * 4_000_000),
        name="attn",
    )(sc, off, own, recv, halo, *sums)


def finish_kernel(sc, off, dq, dkv, *refs):
    tots, outs = refs[:SIDE], refs[SIDE:]
    core, y, z, x = sc[1], sc[2], sc[3], sc[4]
    local = off[y] & 7
    here = (off[y] >> 3) == z
    total = tots[0][...].astype(F32)
    for part in tots[1:]:
        total = total + part[...].astype(F32)
    for step in range(SIDE):
        for side in range(2):
            block = ((core + side) & 1) * SIDE + ((x + step) & 3)
            rows = pl.ds(pl.multiple_of(block * BLOCK, BLOCK), BLOCK)
            value = dkv[:, rows, :] + jnp.where(here & (local == block), total, 0.0)
            outs[step][side, 0] = dq[rows, :]
            outs[step][side, 1:3] = value.astype(BF16)


def finish(sc, off, dq, dkv, tots):
    width = dq.shape[1]
    shape = (2, 3, BLOCK, width)
    return pl.pallas_call(
        finish_kernel,
        grid_spec=pltpu.PrefetchScalarGridSpec(
            num_scalar_prefetch=2,
            grid=(width // HDIM,),
            in_specs=[
                pl.BlockSpec((OWN, HDIM), lambda h, sc, off: (0, h)),
                pl.BlockSpec((2, OWN, HDIM), lambda h, sc, off: (0, 0, h)),
            ]
            + [pl.BlockSpec((2, BLOCK, HDIM), lambda h, sc, off: (0, 0, h))] * SIDE,
            out_specs=[pl.BlockSpec((2, 3, BLOCK, HDIM), lambda h, sc, off: (0, 0, 0, h))] * SIDE,
        ),
        out_shape=[jax.ShapeDtypeStruct(shape, BF16)] * SIDE,
        compiler_params=params(),
        cost_estimate=cost(0, 20 * OWN * width),
        name="finish",
    )(sc, off, dq, dkv, *tots)


def place_kernel(sc, off, *refs):
    groups = len(SIZES)
    outs = refs[(SIDE + 1) * groups :]
    x, core = sc[4], sc[1]
    heads = sum(SIZES)
    at = 0
    for g in range(groups):
        width = SIZES[g] * HDIM
        for step in range(SIDE):
            source = (x + SIDE - step) & 3
            for part in range(2):
                side = core if part == 0 else 1 - core
                first = pl.multiple_of(((source * 2 + side) * heads + at) * HDIM, HDIM)
                ref = refs[g * (SIDE + 1) + (step if part == 0 else SIDE)]
                for n in range(3):
                    outs[n][:, pl.ds(first, width)] = ref[0 if part == 0 else step, n]
        at += SIZES[g]


def place(sc, off, parts):
    columns = sum(SIZES) * HDIM * 2 * SIDE
    shape = (BLOCK, columns)
    specs = []
    for n, p in enumerate(parts):
        lead = SIDE if n % (SIDE + 1) == SIDE else 1
        specs.append(pl.BlockSpec((lead, *p.shape[1:]), lambda i, sc, off: (0, 0, 0, 0)))
    return pl.pallas_call(
        place_kernel,
        grid_spec=pltpu.PrefetchScalarGridSpec(
            num_scalar_prefetch=2,
            grid=(1,),
            in_specs=specs,
            out_specs=[whole(shape)] * 3,
        ),
        out_shape=[jax.ShapeDtypeStruct(shape, BF16)] * 3,
        compiler_params=params(),
        cost_estimate=cost(0, 12 * BLOCK * columns),
        name="place",
    )(sc, off, *parts)


def named(value, pairs, axis="ctx"):
    return lax.ppermute(value, axis, pairs)


def on_device(query, key_in, value_in, dout, off):
    width = query.shape[1]
    me = lax.axis_index("ctx")
    x = lax.axis_index("tp")
    which = lax.iota(jnp.int32, 8)
    sc = jnp.where(which == 0, me >> 1, me & 1)
    sc = jnp.where(which == 2, me >> 3, sc)
    sc = jnp.where(which == 3, (me >> 1) & 3, sc)
    sc = jnp.where(which == 4, x, sc).astype(jnp.int32)
    y, z = me >> 3, (me >> 1) & 3

    own_cand, oth_cand = candidate(sc, off, key_in, value_in)
    pieces = pieces_of(sc, off, own_cand, named(oth_cand, SWAP))
    arrived = [pieces[0]]
    arrived += [named(pieces[n], along_z(n)) for n in range(1, SIDE)]
    step = (z - (off[y] >> 3)) & 3
    piece = arrived[0]
    for n in range(1, SIDE):
        piece = jnp.where(step == n, arrived[n], piece)
    parts = [piece] + [named(piece, along_z(n)) for n in range(1, SIDE)]
    summary = gather(sc, off, parts)
    sums = [summary] + [named(summary, along_y(n)) for n in range(1, NSUM)]

    bases = [sum(SIZES[:g]) for g in range(len(SIZES))]
    work = []
    for g, heads in enumerate(SIZES):
        own, oth = pack(sc, off, (query, dout, key_in, value_in), bases[g], heads, width)
        recv = named(oth, SWAP)
        qd, kv = halo_of(sc, off, own, recv)
        work.append((own, recv, named(kv, ring(1)), named(qd, ring(-1))))

    parts = []
    for g, heads in enumerate(SIZES):
        own, recv, kv, qd = work[g]
        dq, dkv, stat, sent = attn(sc, off, own, recv, kv, sums, bases[g])
        stat = named(stat, ring(-1))
        dkv = later(sc, off, own, recv, qd, stat, dkv)
        part = sent[:, :BLOCK].astype(F32)
        for n in range(1, NSUM):
            moved = named(sent[:, n * BLOCK : (n + 1) * BLOCK], along_y(-n))
            part = part + moved.astype(F32)
        part = part.astype(BF16)
        tots = [part] + [named(part, along_z(n)) for n in range(1, SIDE)]
        cuts = finish(sc, off, dq, dkv, tots)
        there = [cuts[0]]
        there += [named(cuts[n], along_x(n), "tp") for n in range(1, SIDE)]
        parts += there
        parts.append(named(jnp.concatenate([t[1:] for t in there], axis=0), SWAP))
    return tuple(place(sc, off, parts))


def solution(mesh):
    return jax.shard_map(
        on_device,
        mesh=mesh,
        in_specs=(P("ctx", "tp"), P("ctx", "tp"), P("ctx", "tp"), P("ctx", "tp"), P()),
        out_specs=(P(("ctx", "tp"), None),) * 3,
        check_vma=False,
    )
```

```python
import functools
import math

import jax
import jax.numpy as jnp
from jax import lax
from jax.experimental import pallas as pl
from jax.experimental.pallas import tpu as pltpu
from jax.sharding import PartitionSpec as P


HDIM = 128
BLOCK = 128
BAND = 8
STRIDE = 32
CHIP_BLOCKS = 8
HALO = (BAND - 1) * BLOCK
OWN = CHIP_BLOCKS * BLOCK
EXT = HALO + OWN
TILE = 256
NSUM = 4
SPAN = 9
ROWS = (SPAN + NSUM) * BLOCK
NEG = -1e30
SIZES = (3, 3)
CHIPS = 16
SIDE = 4
SCALE = HDIM**-0.5
LOG2E = math.log2(math.e)
BF16 = jnp.bfloat16
F32 = jnp.float32


def ring(step):
    return [(2 * c + k, 2 * ((c + step) % CHIPS) + k) for c in range(CHIPS) for k in range(2)]


def along_z(step):
    return [
        (2 * (y * SIDE + z) + k, 2 * (y * SIDE + (z + step) % SIDE) + k)
        for y in range(SIDE)
        for z in range(SIDE)
        for k in range(2)
    ]


def along_y(step):
    return [
        (2 * (y * SIDE + z) + k, 2 * ((y + step) % SIDE * SIDE + z) + k)
        for y in range(SIDE)
        for z in range(SIDE)
        for k in range(2)
    ]


SWAP = [(d, d ^ 1) for d in range(2 * CHIPS)]


def along_x(step):
    return [(x, (x + step) % SIDE) for x in range(SIDE)]


def params(**kw):
    return pltpu.CompilerParams(vmem_limit_bytes=56 * 1024 * 1024, **kw)


def cost(flops, nbytes):
    return pl.CostEstimate(flops=flops, bytes_accessed=nbytes, transcendentals=0)


def whole(shape):
    return pl.BlockSpec(shape, lambda *_: (0,) * len(shape))


def pack_kernel(sc, off, *refs):
    ins, (own, oth) = refs[:8], refs[8:]
    for n in range(4):
        own[n] = ins[2 * n][...]
        oth[n] = ins[2 * n + 1][...]


def pack(sc, off, arrays, base, heads, width):
    rows = arrays[0].shape[0]
    half = width // HDIM // 2
    chunk = 256
    cols = heads * HDIM
    specs, args = [], []
    for array in arrays:
        for other in (0, 1):
            specs.append(
                pl.BlockSpec(
                    (chunk, cols),
                    lambda i, sc, off, other=other: (
                        i,
                        jnp.abs(sc[1] - other) * (half // heads) + base // heads,
                    ),
                )
            )
            args.append(array)
    out = pl.BlockSpec((4, chunk, cols), lambda i, sc, off: (0, i, 0))
    shape = jax.ShapeDtypeStruct((4, rows, cols), BF16)
    return pl.pallas_call(
        pack_kernel,
        grid_spec=pltpu.PrefetchScalarGridSpec(
            num_scalar_prefetch=2,
            grid=(rows // chunk,),
            in_specs=specs,
            out_specs=[out, out],
        ),
        out_shape=[shape, shape],
        compiler_params=params(),
        cost_estimate=cost(0, 16 * rows * cols * 2),
        name="pack",
    )(sc, off, *args)


def halo_kernel(sc, off, own, recv, qd, kv):
    lo = OWN // 2

    def fill(first, second):
        @pl.when(pl.program_id(0) < 2)
        def _():
            qd[:, :lo] = first[...]
            qd[:, lo:] = second[:, : lo - BLOCK]

        @pl.when(pl.program_id(0) >= 2)
        def _():
            kv[:, : lo - BLOCK] = first[:, BLOCK:]
            kv[:, lo - BLOCK :] = second[...]

    pl.when(sc[1] == 0)(lambda: fill(own, recv))
    pl.when(sc[1] == 1)(lambda: fill(recv, own))


def halo_of(sc, off, own, recv):
    width = own.shape[2]
    spec = pl.BlockSpec((1, OWN // 2, width), lambda i, sc, off: (i, 0, 0))
    return pl.pallas_call(
        halo_kernel,
        grid_spec=pltpu.PrefetchScalarGridSpec(
            num_scalar_prefetch=2,
            grid=(4,),
            in_specs=[spec, spec],
            out_specs=[
                pl.BlockSpec((1, HALO, width), lambda i, sc, off: (jnp.minimum(i, 1), 0, 0)),
                pl.BlockSpec((1, HALO, width), lambda i, sc, off: (jnp.maximum(i - 2, 0), 0, 0)),
            ],
        ),
        out_shape=[jax.ShapeDtypeStruct((2, HALO, width), BF16)] * 2,
        compiler_params=params(),
        cost_estimate=cost(0, 16 * OWN * width * 2),
        name="halo",
    )(sc, off, own, recv)


def candidate_kernel(sc, off, key, value, own, oth):
    half = own.shape[2]
    for n, ref in enumerate((key, value)):
        own[n] = ref[:, pl.ds(pl.multiple_of(sc[1] * half, HDIM), half)]
        oth[n] = ref[:, pl.ds(pl.multiple_of((1 - sc[1]) * half, HDIM), half)]


def candidate(sc, off, key, value):
    width = key.shape[1]
    spec = pl.BlockSpec((BLOCK, width), lambda i, sc, off: (off[sc[2]] & 3, 0))
    shape = (2, BLOCK, width // 2)
    return pl.pallas_call(
        candidate_kernel,
        grid_spec=pltpu.PrefetchScalarGridSpec(
            num_scalar_prefetch=2, grid=(1,), in_specs=[spec] * 2, out_specs=[whole(shape)] * 2
        ),
        out_shape=[jax.ShapeDtypeStruct(shape, BF16)] * 2,
        compiler_params=params(),
        cost_estimate=cost(0, 8 * BLOCK * width),
        name="candidate",
    )(sc, off, key, value)


def pieces_kernel(sc, off, own, recv, *outs):
    piece = BLOCK // SIDE
    mine = ((off[sc[2]] & 7) >> 2) == sc[1]
    for step in range(SIDE):
        row = pl.multiple_of(((sc[3] + step) & 3) * piece, piece)

        def put(ref, out=outs[step], row=row):
            out[...] = ref[:, pl.ds(row, piece), :]

        pl.when(mine)(functools.partial(put, own))
        pl.when(jnp.logical_not(mine))(functools.partial(put, recv))


def pieces_of(sc, off, own, recv):
    shape = (2, BLOCK // SIDE, own.shape[2])
    return pl.pallas_call(
        pieces_kernel,
        grid_spec=pltpu.PrefetchScalarGridSpec(
            num_scalar_prefetch=2,
            grid=(1,),
            in_specs=[whole(own.shape)] * 2,
            out_specs=[whole(shape)] * SIDE,
        ),
        out_shape=[jax.ShapeDtypeStruct(shape, BF16)] * SIDE,
        compiler_params=params(),
        cost_estimate=cost(0, 8 * own.size),
        name="pieces",
    )(sc, off, own, recv)


def gather_kernel(sc, off, *refs):
    out = refs[SIDE]
    piece = BLOCK // SIDE
    for step in range(SIDE):
        row = pl.multiple_of(((sc[3] + SIDE - step) % SIDE) * piece, piece)
        out[:, pl.ds(row, piece), :] = refs[step][...]


def gather(sc, off, pieces):
    shape = pieces[0].shape
    full = (2, BLOCK, shape[2])
    return pl.pallas_call(
        gather_kernel,
        grid_spec=pltpu.PrefetchScalarGridSpec(
            num_scalar_prefetch=2, grid=(1,), in_specs=[whole(shape)] * SIDE, out_specs=whole(full)
        ),
        out_shape=jax.ShapeDtypeStruct(full, BF16),
        compiler_params=params(),
        cost_estimate=cost(0, 4 * BLOCK * shape[2] * 2),
        name="gather",
    )(sc, off, *pieces)


def fold(x, op):
    return op(x.reshape(x.shape[0] // 8, 8, x.shape[1]), axis=0)


def spread(x):
    return x.reshape(x.shape[0] // 8, 8, x.shape[1])


def dot_nt(a, b):
    return lax.dot_general(a, b, (((1,), (1,)), ((), ())), preferred_element_type=F32)


def dot_nn(a, b):
    return lax.dot_general(a, b, (((1,), (0,)), ((), ())), preferred_element_type=F32)


def load_own(buf, own, recv, core, n, start):
    half = OWN // 2
    buf[pl.ds(pl.multiple_of(start + core * half, BLOCK), half), :] = own[n]
    buf[pl.ds(pl.multiple_of(start + (1 - core) * half, BLOCK), half), :] = recv[n]


def attn_kernel(sc, off, own, recv, halo, s0, s1, s2, s3, dq, dkv, stat, ds_out, *scratch):
    kx, vx, qs, dos, kxt, xs, dps, dsb, pb = scratch
    core, chip, y = sc[1], sc[0], sc[2]
    load_own(qs, own, recv, core, 0, 0)
    load_own(dos, own, recv, core, 1, 0)
    for buf, n in ((kx, 0), (vx, 1)):
        buf[0:HALO, :] = halo[n]
        load_own(buf, own, recv, core, 2 + n, HALO)
        for s, part in enumerate((s0, s1, s2, s3)):
            buf[EXT + s * BLOCK : EXT + (s + 1) * BLOCK, :] = part[n]
    kxt[...] = kx[...].T
    row = lax.broadcasted_iota(jnp.int32, (BLOCK, TILE), 0)
    col = lax.broadcasted_iota(jnp.int32, (BLOCK, TILE), 1)
    first = lax.broadcasted_iota(jnp.int32, (1, TILE), 1) < BLOCK
    outside = jnp.where(chip == 0, NEG, 0.0)

    for t in range(OWN // TILE):
        base = t * TILE
        q_t = qs[base : base + TILE, :]
        do_t = dos[base : base + TILE, :]

        def start_of(j, base=base):
            return base + j * BLOCK if j < SPAN else EXT + (j - SPAN) * BLOCK

        m8 = jnp.full((8, TILE), NEG, F32)
        l8 = jnp.zeros((8, TILE), F32)
        d8 = jnp.zeros((8, TILE), F32)
        tops = []
        for j in range(SPAN + NSUM):
            span = slice(j * BLOCK, (j + 1) * BLOCK)
            at = slice(start_of(j), start_of(j) + BLOCK)
            x = dot_nt(kx[at, :], q_t) * (SCALE * LOG2E)
            if start_of(j) < HALO:
                x = x + outside
            if j == 0:
                x = jnp.where(first, x, NEG)
            if j == BAND - 1:
                x = jnp.where(row <= col, x, NEG)
            if j == BAND:
                x = jnp.where(row + BLOCK <= col, x, NEG)
            if j >= SPAN:
                slot = (y + NSUM - (j - SPAN)) & 3
                g = slot * STRIDE + off[slot]
                block = chip * CHIP_BLOCKS + 2 * t - (BAND - 1)
                b0 = jnp.where(g < block, 0.0, NEG)
                b1 = jnp.where(g < block + 1, 0.0, NEG)
                x = x + jnp.where(first, b0, b1)
            dp = dot_nt(vx[at, :], do_t)
            top = jnp.maximum(m8, fold(x, jnp.max))
            fade = jnp.exp2(m8 - top)
            p = jnp.exp2(spread(x) - top[None])
            l8 = l8 * fade + jnp.sum(p, axis=0)
            d8 = d8 * fade + jnp.sum(p * spread(dp), axis=0)
            xs[span, :] = p.reshape(BLOCK, TILE)
            dps[span, :] = dp
            m8 = top
            tops.append(top)
        m = jnp.max(m8, axis=0, keepdims=True)
        rest = jnp.exp2(m8 - m)
        total = jnp.sum(l8 * rest, axis=0, keepdims=True)
        inv = 1.0 / total
        delta = jnp.sum(d8 * rest, axis=0, keepdims=True) * inv
        stat[0, 0:1, base : base + TILE] = m + jnp.log2(total)
        stat[0, 1:2, base : base + TILE] = delta
        for j in range(SPAN + NSUM):
            span = slice(j * BLOCK, (j + 1) * BLOCK)
            factor = jnp.exp2(tops[j] - m) * inv
            p = (spread(xs[span, :]) * factor[None]).reshape(BLOCK, TILE)
            at = start_of(j)
            cols = slice(base, base + TILE)
            dsb[at : at + BLOCK, cols] = (p * (dps[span, :] - delta)).astype(BF16)
            if at >= HALO:
                pb[at - HALO : at - HALO + BLOCK, cols] = p.astype(BF16)
        cols = slice(base, base + TILE)
        dqt = dot_nn(kxt[:, base : base + SPAN * BLOCK], dsb[base : base + SPAN * BLOCK, cols])
        dqt = dqt + dot_nn(kxt[:, EXT:], dsb[EXT:, cols])
        dq[base : base + TILE, :] = (dqt * SCALE).T.astype(BF16)

    for t in range(OWN // TILE):
        keys = slice(t * TILE, (t + 1) * TILE)
        dkv[0, keys, :] = dot_nn(dsb[HALO + t * TILE : HALO + (t + 1) * TILE, t * TILE :], qs[t * TILE :, :])
        dkv[1, keys, :] = dot_nn(pb[keys, t * TILE :], dos[t * TILE :, :])
    for s in range(NSUM // 2):
        keys = slice(s * TILE, (s + 1) * TILE)
        ds_out[0, keys, :] = (
            dot_nn(dsb[EXT + s * TILE : EXT + (s + 1) * TILE, :], qs[...]) * SCALE
        ).astype(BF16)
        ds_out[1, keys, :] = dot_nn(pb[OWN + s * TILE : OWN + (s + 1) * TILE, :], dos[...]).astype(BF16)


def later_kernel(sc, off, own, recv, qd, stat, dkv, out, kx, vx, qs, dos, dsb, pb):
    core, chip = sc[1], sc[0]
    load_own(kx, own, recv, core, 0, 0)
    load_own(vx, own, recv, core, 1, 0)
    for buf, n in ((qs, 0), (dos, 1)):
        buf[0:HALO, :] = qd[n]
        buf[HALO:, :] = jnp.zeros((OWN - HALO, HDIM), BF16)
    first = lax.broadcasted_iota(jnp.int32, (1, TILE), 1) < BLOCK
    outside = jnp.where(chip == CHIPS - 1, NEG, 0.0)
    for t in range(OWN // TILE):
        cols = slice(t * TILE, (t + 1) * TILE)
        q_t = qs[cols, :]
        do_t = dos[cols, :]
        shift = outside - stat[0, 0:1, cols]
        delta = stat[0, 1:2, cols]
        for j in range(2 * t + 1, CHIP_BLOCKS):
            at = slice(j * BLOCK, (j + 1) * BLOCK)
            x = dot_nt(kx[at, :], q_t) * (SCALE * LOG2E) + shift
            if j == 2 * t + 1:
                x = jnp.where(first, x, NEG)
            p = jnp.exp2(x)
            dsb[at, cols] = (p * (dot_nt(vx[at, :], do_t) - delta)).astype(BF16)
            pb[at, cols] = p.astype(BF16)
    for j in range(0, CHIP_BLOCKS):
        at = slice(j * BLOCK, (j + 1) * BLOCK)
        upto = (j + 1) // 2 * TILE
        for n, (low, rows, by) in enumerate(((dsb, qs, SCALE), (pb, dos, 1.0))):
            value = dkv[n, at, :]
            if upto:
                value = value + dot_nn(low[at, :upto], rows[:upto, :])
            out[n, at, :] = value * by


def later(sc, off, own, recv, qd, stat, dkv):
    width = own.shape[2]
    heads = width // HDIM
    pair = pl.BlockSpec((2, OWN // 2, HDIM), lambda h, sc, off: (1, 0, h))
    full = pl.BlockSpec((2, OWN, HDIM), lambda h, sc, off: (0, 0, h))
    return pl.pallas_call(
        later_kernel,
        grid_spec=pltpu.PrefetchScalarGridSpec(
            num_scalar_prefetch=2,
            grid=(heads,),
            in_specs=[
                pair,
                pair,
                pl.BlockSpec((2, HALO, HDIM), lambda h, sc, off: (0, 0, h)),
                pl.BlockSpec((1, 8, OWN), lambda h, sc, off: (h, 0, 0)),
                full,
            ],
            out_specs=full,
            scratch_shapes=[pltpu.VMEM((OWN, HDIM), BF16)] * 4 + [pltpu.VMEM((OWN, OWN), BF16)] * 2,
        ),
        out_shape=jax.ShapeDtypeStruct((2, OWN, width), F32),
        compiler_params=params(),
        cost_estimate=cost(heads * 28 * 8 * 128**3 * 2, heads * 4_000_000),
        name="later",
    )(sc, off, own, recv, qd, stat, dkv)


def attn(sc, off, own, recv, halo, sums, base):
    width = own.shape[2]
    heads = width // HDIM
    keys = EXT + NSUM * BLOCK

    def by_head(n, rows):
        return pl.BlockSpec((n, rows, HDIM), lambda h, sc, off: (0, 0, h))

    sum_spec = pl.BlockSpec((2, BLOCK, HDIM), lambda h, sc, off: (0, 0, base + h))
    return pl.pallas_call(
        attn_kernel,
        grid_spec=pltpu.PrefetchScalarGridSpec(
            num_scalar_prefetch=2,
            grid=(heads,),
            in_specs=[by_head(4, OWN // 2), by_head(4, OWN // 2), by_head(2, HALO)]
            + [sum_spec] * NSUM,
            out_specs=[
                pl.BlockSpec((OWN, HDIM), lambda h, sc, off: (0, h)),
                by_head(2, OWN),
                pl.BlockSpec((1, 8, OWN), lambda h, sc, off: (h, 0, 0)),
                by_head(2, NSUM * BLOCK),
            ],
            scratch_shapes=[
                pltpu.VMEM((keys, HDIM), BF16),
                pltpu.VMEM((keys, HDIM), BF16),
                pltpu.VMEM((OWN, HDIM), BF16),
                pltpu.VMEM((OWN, HDIM), BF16),
                pltpu.VMEM((HDIM, keys), BF16),
                pltpu.VMEM((ROWS, TILE), F32),
                pltpu.VMEM((ROWS, TILE), F32),
                pltpu.VMEM((keys, OWN), BF16),
                pltpu.VMEM((OWN + NSUM * BLOCK, OWN), BF16),
            ],
        ),
        out_shape=[
            jax.ShapeDtypeStruct((OWN, width), BF16),
            jax.ShapeDtypeStruct((2, OWN, width), F32),
            jax.ShapeDtypeStruct((heads, 8, OWN), F32),
            jax.ShapeDtypeStruct((2, NSUM * BLOCK, width), BF16),
        ],
        compiler_params=params(),
        cost_estimate=cost(heads * 96 * 10 * 128**3 * 2, heads * 4_000_000),
        name="attn",
    )(sc, off, own, recv, halo, *sums)


def finish_kernel(sc, off, dkv, *refs):
    tots, outs = refs[:SIDE], refs[SIDE:]
    core, y, z, x = sc[1], sc[2], sc[3], sc[4]
    local = off[y] & 7
    here = (off[y] >> 3) == z
    total = tots[0][...].astype(F32)
    for part in tots[1:]:
        total = total + part[...].astype(F32)
    for step in range(SIDE):
        for side in range(2):
            block = ((core + side) & 1) * SIDE + ((x + step) & 3)
            rows = pl.ds(pl.multiple_of(block * BLOCK, BLOCK), BLOCK)
            value = dkv[:, rows, :] + jnp.where(here & (local == block), total, 0.0)
            outs[step][side] = value.astype(BF16)


def finish(sc, off, dkv, tots, base):
    width = dkv.shape[2]
    shape = (2, 2, BLOCK, width)
    return pl.pallas_call(
        finish_kernel,
        grid_spec=pltpu.PrefetchScalarGridSpec(
            num_scalar_prefetch=2,
            grid=(width // HDIM,),
            in_specs=[pl.BlockSpec((2, OWN, HDIM), lambda h, sc, off: (0, 0, h))]
            + [pl.BlockSpec((2, BLOCK, HDIM), lambda h, sc, off: (0, 0, base + h))] * SIDE,
            out_specs=[pl.BlockSpec((2, 2, BLOCK, HDIM), lambda h, sc, off: (0, 0, 0, h))] * SIDE,
        ),
        out_shape=[jax.ShapeDtypeStruct(shape, BF16)] * SIDE,
        compiler_params=params(),
        cost_estimate=cost(0, 16 * OWN * width),
        name="finish",
    )(sc, off, dkv, *tots)


def cut_kernel(sc, off, *refs):
    core, x = sc[1], sc[4]
    ins, outs = refs[: len(SIZES)], refs[len(SIZES) :]
    for step in range(SIDE):
        for side in range(2):
            block = ((core + side) & 1) * SIDE + ((x + step) & 3)
            rows = pl.ds(pl.multiple_of(block * BLOCK, BLOCK), BLOCK)
            at = 0
            for ref, heads in zip(ins, SIZES):
                outs[step][side, 0, :, at : at + heads * HDIM] = ref[rows, :]
                at += heads * HDIM


def cut(sc, off, dqs):
    shape = (2, 1, BLOCK, sum(SIZES) * HDIM)
    return pl.pallas_call(
        cut_kernel,
        grid_spec=pltpu.PrefetchScalarGridSpec(
            num_scalar_prefetch=2,
            grid=(1,),
            in_specs=[whole(dq.shape) for dq in dqs],
            out_specs=[whole(shape)] * SIDE,
        ),
        out_shape=[jax.ShapeDtypeStruct(shape, BF16)] * SIDE,
        compiler_params=params(),
        cost_estimate=cost(0, 4 * OWN * shape[3]),
        name="cut",
    )(sc, off, *dqs)


def place_kernel(sizes, sc, off, *refs):
    outs = refs[(SIDE + 1) * len(sizes) :]
    x, core = sc[4], sc[1]
    heads = sum(sizes)
    at = 0
    for g, size in enumerate(sizes):
        width = size * HDIM
        for step in range(SIDE):
            source = (x + SIDE - step) & 3
            for part in range(2):
                side = core if part == 0 else 1 - core
                first = pl.multiple_of(((source * 2 + side) * heads + at) * HDIM, HDIM)
                ref = refs[g * (SIDE + 1) + (step if part == 0 else SIDE)]
                for n, out in enumerate(outs):
                    out[:, pl.ds(first, width)] = ref[0 if part == 0 else step, n]
        at += size


def place(sc, off, parts, count, sizes):
    columns = sum(sizes) * HDIM * 2 * SIDE
    shape = (BLOCK, columns)
    specs = []
    for n, p in enumerate(parts):
        lead = SIDE if n % (SIDE + 1) == SIDE else 1
        specs.append(pl.BlockSpec((lead, *p.shape[1:]), lambda i, sc, off: (0, 0, 0, 0)))
    return pl.pallas_call(
        functools.partial(place_kernel, sizes),
        grid_spec=pltpu.PrefetchScalarGridSpec(
            num_scalar_prefetch=2,
            grid=(1,),
            in_specs=specs,
            out_specs=[whole(shape)] * count,
        ),
        out_shape=[jax.ShapeDtypeStruct(shape, BF16)] * count,
        compiler_params=params(),
        cost_estimate=cost(0, 4 * count * BLOCK * columns),
        name="place",
    )(sc, off, *parts)


def spread_out(cuts):
    there = [cuts[0]]
    there += [named(cuts[n], along_x(n), "tp") for n in range(1, SIDE)]
    return there + [named(jnp.concatenate([t[1:] for t in there], axis=0), SWAP)]


def named(value, pairs, axis="ctx"):
    return lax.ppermute(value, axis, pairs)


def on_device(query, key_in, value_in, dout, off):
    width = query.shape[1]
    me = lax.axis_index("ctx")
    x = lax.axis_index("tp")
    which = lax.iota(jnp.int32, 8)
    sc = jnp.where(which == 0, me >> 1, me & 1)
    sc = jnp.where(which == 2, me >> 3, sc)
    sc = jnp.where(which == 3, (me >> 1) & 3, sc)
    sc = jnp.where(which == 4, x, sc).astype(jnp.int32)
    y, z = me >> 3, (me >> 1) & 3

    own_cand, oth_cand = candidate(sc, off, key_in, value_in)
    pieces = pieces_of(sc, off, own_cand, named(oth_cand, SWAP))
    arrived = [pieces[0]]
    arrived += [named(pieces[n], along_z(n)) for n in range(1, SIDE)]
    step = (z - (off[y] >> 3)) & 3
    piece = arrived[0]
    for n in range(1, SIDE):
        piece = jnp.where(step == n, arrived[n], piece)
    parts = [piece] + [named(piece, along_z(n)) for n in range(1, SIDE)]
    summary = gather(sc, off, parts)
    sums = [summary] + [named(summary, along_y(n)) for n in range(1, NSUM)]

    bases = [sum(SIZES[:g]) for g in range(len(SIZES))]
    work = []
    for g, heads in enumerate(SIZES):
        own, oth = pack(sc, off, (query, dout, key_in, value_in), bases[g], heads, width)
        recv = named(oth, SWAP)
        qd, kv = halo_of(sc, off, own, recv)
        work.append((own, recv, named(kv, ring(1)), named(qd, ring(-1))))

    dqs, sents, dkvs, stats = [], [], [], []
    for g in range(len(SIZES)):
        own, recv, kv, qd = work[g]
        dq, dkv, stat, sent = attn(sc, off, own, recv, kv, sums, bases[g])
        stats.append(named(stat, ring(-1)))
        dqs.append(dq)
        dkvs.append(dkv)
        sents.append(sent)
    sent = jnp.concatenate(sents, axis=2)
    part = sent[:, :BLOCK].astype(F32)
    for n in range(1, NSUM):
        moved = named(sent[:, n * BLOCK : (n + 1) * BLOCK], along_y(-n))
        part = part + moved.astype(F32)
    part = part.astype(BF16)
    tots = [part] + [named(part, along_z(n)) for n in range(1, SIDE)]
    cuts = cut(sc, off, dqs)
    grad_q = place(sc, off, spread_out(cuts), 1, (sum(SIZES),))
    parts = []
    for g in range(len(SIZES)):
        own, recv, kv, qd = work[g]
        dkv = later(sc, off, own, recv, qd, stats[g], dkvs[g])
        cuts = finish(sc, off, dkv, tots, bases[g])
        parts += spread_out(cuts)
    return (*grad_q, *place(sc, off, parts, 2, SIZES))


def solution(mesh):
    return jax.shard_map(
        on_device,
        mesh=mesh,
        in_specs=(P("ctx", "tp"), P("ctx", "tp"), P("ctx", "tp"), P("ctx", "tp"), P()),
        out_specs=(P(("ctx", "tp"), None),) * 3,
        check_vma=False,
    )
```

```python
import functools
import math

import jax
import jax.numpy as jnp
from jax import lax
from jax.experimental import pallas as pl
from jax.experimental.pallas import tpu as pltpu
from jax.sharding import PartitionSpec as P


HDIM = 128
BLOCK = 128
BAND = 8
STRIDE = 32
CHIP_BLOCKS = 8
HALO = (BAND - 1) * BLOCK
OWN = CHIP_BLOCKS * BLOCK
EXT = HALO + OWN
TILE = 256
NSUM = 4
SPAN = 9
ROWS = (SPAN + NSUM) * BLOCK
NEG = -1e30
SIZES = (3, 3)
CHIPS = 16
SIDE = 4
SCALE = HDIM**-0.5
LOG2E = math.log2(math.e)
BF16 = jnp.bfloat16
F32 = jnp.float32


def ring(step):
    return [(2 * c + k, 2 * ((c + step) % CHIPS) + k) for c in range(CHIPS) for k in range(2)]


def along_z(step):
    return [
        (2 * (y * SIDE + z) + k, 2 * (y * SIDE + (z + step) % SIDE) + k)
        for y in range(SIDE)
        for z in range(SIDE)
        for k in range(2)
    ]


def along_y(step):
    return [
        (2 * (y * SIDE + z) + k, 2 * ((y + step) % SIDE * SIDE + z) + k)
        for y in range(SIDE)
        for z in range(SIDE)
        for k in range(2)
    ]


SWAP = [(d, d ^ 1) for d in range(2 * CHIPS)]


def along_x(step):
    return [(x, (x + step) % SIDE) for x in range(SIDE)]


def params(**kw):
    return pltpu.CompilerParams(vmem_limit_bytes=56 * 1024 * 1024, **kw)


def cost(flops, nbytes):
    return pl.CostEstimate(flops=flops, bytes_accessed=nbytes, transcendentals=0)


def whole(shape):
    return pl.BlockSpec(shape, lambda *_: (0,) * len(shape))


def pack_kernel(sc, off, *refs):
    ins, (own, oth) = refs[:8], refs[8:]
    for n in range(4):
        own[n] = ins[2 * n][...]
        oth[n] = ins[2 * n + 1][...]


def pack(sc, off, arrays, base, heads, width):
    rows = arrays[0].shape[0]
    half = width // HDIM // 2
    chunk = 256
    cols = heads * HDIM
    specs, args = [], []
    for array in arrays:
        for other in (0, 1):
            specs.append(
                pl.BlockSpec(
                    (chunk, cols),
                    lambda i, sc, off, other=other: (
                        i,
                        jnp.abs(sc[1] - other) * (half // heads) + base // heads,
                    ),
                )
            )
            args.append(array)
    out = pl.BlockSpec((4, chunk, cols), lambda i, sc, off: (0, i, 0))
    shape = jax.ShapeDtypeStruct((4, rows, cols), BF16)
    return pl.pallas_call(
        pack_kernel,
        grid_spec=pltpu.PrefetchScalarGridSpec(
            num_scalar_prefetch=2,
            grid=(rows // chunk,),
            in_specs=specs,
            out_specs=[out, out],
        ),
        out_shape=[shape, shape],
        compiler_params=params(),
        cost_estimate=cost(0, 16 * rows * cols * 2),
        name="pack",
    )(sc, off, *args)


def halo_kernel(sc, off, own, recv, qd, kv):
    lo = OWN // 2

    def fill(first, second):
        @pl.when(pl.program_id(0) < 2)
        def _():
            qd[:, :lo] = first[...]
            qd[:, lo:] = second[:, : lo - BLOCK]

        @pl.when(pl.program_id(0) >= 2)
        def _():
            kv[:, : lo - BLOCK] = first[:, BLOCK:]
            kv[:, lo - BLOCK :] = second[...]

    pl.when(sc[1] == 0)(lambda: fill(own, recv))
    pl.when(sc[1] == 1)(lambda: fill(recv, own))


def halo_of(sc, off, own, recv):
    width = own.shape[2]
    spec = pl.BlockSpec((1, OWN // 2, width), lambda i, sc, off: (i, 0, 0))
    return pl.pallas_call(
        halo_kernel,
        grid_spec=pltpu.PrefetchScalarGridSpec(
            num_scalar_prefetch=2,
            grid=(4,),
            in_specs=[spec, spec],
            out_specs=[
                pl.BlockSpec((1, HALO, width), lambda i, sc, off: (jnp.minimum(i, 1), 0, 0)),
                pl.BlockSpec((1, HALO, width), lambda i, sc, off: (jnp.maximum(i - 2, 0), 0, 0)),
            ],
        ),
        out_shape=[jax.ShapeDtypeStruct((2, HALO, width), BF16)] * 2,
        compiler_params=params(),
        cost_estimate=cost(0, 16 * OWN * width * 2),
        name="halo",
    )(sc, off, own, recv)


def candidate_kernel(sc, off, key, value, own, oth):
    half = own.shape[2]
    for n, ref in enumerate((key, value)):
        own[n] = ref[:, pl.ds(pl.multiple_of(sc[1] * half, HDIM), half)]
        oth[n] = ref[:, pl.ds(pl.multiple_of((1 - sc[1]) * half, HDIM), half)]


def candidate(sc, off, key, value):
    width = key.shape[1]
    spec = pl.BlockSpec((BLOCK, width), lambda i, sc, off: (off[sc[2]] & 3, 0))
    shape = (2, BLOCK, width // 2)
    return pl.pallas_call(
        candidate_kernel,
        grid_spec=pltpu.PrefetchScalarGridSpec(
            num_scalar_prefetch=2, grid=(1,), in_specs=[spec] * 2, out_specs=[whole(shape)] * 2
        ),
        out_shape=[jax.ShapeDtypeStruct(shape, BF16)] * 2,
        compiler_params=params(),
        cost_estimate=cost(0, 8 * BLOCK * width),
        name="candidate",
    )(sc, off, key, value)


def pieces_kernel(sc, off, own, recv, *outs):
    piece = BLOCK // SIDE
    mine = ((off[sc[2]] & 7) >> 2) == sc[1]
    for step in range(SIDE):
        row = pl.multiple_of(((sc[3] + step) & 3) * piece, piece)

        def put(ref, out=outs[step], row=row):
            out[...] = ref[:, pl.ds(row, piece), :]

        pl.when(mine)(functools.partial(put, own))
        pl.when(jnp.logical_not(mine))(functools.partial(put, recv))


def pieces_of(sc, off, own, recv):
    shape = (2, BLOCK // SIDE, own.shape[2])
    return pl.pallas_call(
        pieces_kernel,
        grid_spec=pltpu.PrefetchScalarGridSpec(
            num_scalar_prefetch=2,
            grid=(1,),
            in_specs=[whole(own.shape)] * 2,
            out_specs=[whole(shape)] * SIDE,
        ),
        out_shape=[jax.ShapeDtypeStruct(shape, BF16)] * SIDE,
        compiler_params=params(),
        cost_estimate=cost(0, 8 * own.size),
        name="pieces",
    )(sc, off, own, recv)


def gather_kernel(sc, off, *refs):
    out = refs[SIDE]
    piece = BLOCK // SIDE
    for step in range(SIDE):
        row = pl.multiple_of(((sc[3] + SIDE - step) % SIDE) * piece, piece)
        out[:, pl.ds(row, piece), :] = refs[step][...]


def gather(sc, off, pieces):
    shape = pieces[0].shape
    full = (2, BLOCK, shape[2])
    return pl.pallas_call(
        gather_kernel,
        grid_spec=pltpu.PrefetchScalarGridSpec(
            num_scalar_prefetch=2, grid=(1,), in_specs=[whole(shape)] * SIDE, out_specs=whole(full)
        ),
        out_shape=jax.ShapeDtypeStruct(full, BF16),
        compiler_params=params(),
        cost_estimate=cost(0, 4 * BLOCK * shape[2] * 2),
        name="gather",
    )(sc, off, *pieces)


def fold(x, op):
    return op(x.reshape(x.shape[0] // 8, 8, x.shape[1]), axis=0)


def spread(x):
    return x.reshape(x.shape[0] // 8, 8, x.shape[1])


def dot_nt(a, b):
    return lax.dot_general(a, b, (((1,), (1,)), ((), ())), preferred_element_type=F32)


def dot_nn(a, b):
    return lax.dot_general(a, b, (((1,), (0,)), ((), ())), preferred_element_type=F32)


def load_own(buf, own, recv, core, n, start):
    half = OWN // 2
    buf[pl.ds(pl.multiple_of(start + core * half, BLOCK), half), :] = own[n]
    buf[pl.ds(pl.multiple_of(start + (1 - core) * half, BLOCK), half), :] = recv[n]


def attn_kernel(sc, off, own, recv, halo, s0, s1, s2, s3, dq, dkv, stat, ds_out, *scratch):
    kx, vx, qs, dos, kxt, xs, dps, dsb, pb = scratch
    core, chip, y = sc[1], sc[0], sc[2]
    load_own(qs, own, recv, core, 0, 0)
    load_own(dos, own, recv, core, 1, 0)
    for buf, n in ((kx, 0), (vx, 1)):
        buf[0:HALO, :] = halo[n]
        load_own(buf, own, recv, core, 2 + n, HALO)
        for s, part in enumerate((s0, s1, s2, s3)):
            buf[EXT + s * BLOCK : EXT + (s + 1) * BLOCK, :] = part[n]
    kxt[...] = kx[...].T
    row = lax.broadcasted_iota(jnp.int32, (BLOCK, TILE), 0)
    col = lax.broadcasted_iota(jnp.int32, (BLOCK, TILE), 1)
    first = lax.broadcasted_iota(jnp.int32, (1, TILE), 1) < BLOCK
    outside = jnp.where(chip == 0, NEG, 0.0)

    for t in range(OWN // TILE):
        base = t * TILE
        q_t = qs[base : base + TILE, :]
        do_t = dos[base : base + TILE, :]

        def start_of(j, base=base):
            return base + j * BLOCK if j < SPAN else EXT + (j - SPAN) * BLOCK

        m8 = jnp.full((8, TILE), NEG, F32)
        l8 = jnp.zeros((8, TILE), F32)
        d8 = jnp.zeros((8, TILE), F32)
        tops = []
        for j in range(SPAN + NSUM):
            span = slice(j * BLOCK, (j + 1) * BLOCK)
            at = slice(start_of(j), start_of(j) + BLOCK)
            x = dot_nt(kx[at, :], q_t) * (SCALE * LOG2E)
            if start_of(j) < HALO:
                x = x + outside
            if j == 0:
                x = jnp.where(first, x, NEG)
            if j == BAND - 1:
                x = jnp.where(row <= col, x, NEG)
            if j == BAND:
                x = jnp.where(row + BLOCK <= col, x, NEG)
            if j >= SPAN:
                slot = (y + NSUM - (j - SPAN)) & 3
                g = slot * STRIDE + off[slot]
                block = chip * CHIP_BLOCKS + 2 * t - (BAND - 1)
                b0 = jnp.where(g < block, 0.0, NEG)
                b1 = jnp.where(g < block + 1, 0.0, NEG)
                x = x + jnp.where(first, b0, b1)
            dp = dot_nt(vx[at, :], do_t)
            top = jnp.maximum(m8, fold(x, jnp.max))
            fade = jnp.exp2(m8 - top)
            p = jnp.exp2(spread(x) - top[None])
            l8 = l8 * fade + jnp.sum(p, axis=0)
            d8 = d8 * fade + jnp.sum(p * spread(dp), axis=0)
            xs[span, :] = p.reshape(BLOCK, TILE)
            dps[span, :] = dp
            m8 = top
            tops.append(top)
        m = jnp.max(m8, axis=0, keepdims=True)
        rest = jnp.exp2(m8 - m)
        total = jnp.sum(l8 * rest, axis=0, keepdims=True)
        inv = 1.0 / total
        delta = jnp.sum(d8 * rest, axis=0, keepdims=True) * inv
        stat[0, 0:1, base : base + TILE] = m + jnp.log2(total)
        stat[0, 1:2, base : base + TILE] = delta
        for j in range(SPAN + NSUM):
            span = slice(j * BLOCK, (j + 1) * BLOCK)
            factor = jnp.exp2(tops[j] - m) * inv
            p = (spread(xs[span, :]) * factor[None]).reshape(BLOCK, TILE)
            at = start_of(j)
            cols = slice(base, base + TILE)
            dsb[at : at + BLOCK, cols] = (p * (dps[span, :] - delta)).astype(BF16)
            if at >= HALO:
                pb[at - HALO : at - HALO + BLOCK, cols] = p.astype(BF16)
        cols = slice(base, base + TILE)
        dqt = dot_nn(kxt[:, base : base + SPAN * BLOCK], dsb[base : base + SPAN * BLOCK, cols])
        dqt = dqt + dot_nn(kxt[:, EXT:], dsb[EXT:, cols])
        dq[base : base + TILE, :] = (dqt * SCALE).T.astype(BF16)

    for t in range(OWN // TILE):
        keys = slice(t * TILE, (t + 1) * TILE)
        dkv[0, keys, :] = dot_nn(dsb[HALO + t * TILE : HALO + (t + 1) * TILE, t * TILE :], qs[t * TILE :, :])
        dkv[1, keys, :] = dot_nn(pb[keys, t * TILE :], dos[t * TILE :, :])
    for s in range(NSUM // 2):
        keys = slice(s * TILE, (s + 1) * TILE)
        ds_out[0, keys, :] = (
            dot_nn(dsb[EXT + s * TILE : EXT + (s + 1) * TILE, :], qs[...]) * SCALE
        ).astype(BF16)
        ds_out[1, keys, :] = dot_nn(pb[OWN + s * TILE : OWN + (s + 1) * TILE, :], dos[...]).astype(BF16)


def later_kernel(sc, off, own, recv, qd, stat, dkv, out, kx, vx, qs, dos, dsb, pb):
    core, chip = sc[1], sc[0]
    load_own(kx, own, recv, core, 0, 0)
    load_own(vx, own, recv, core, 1, 0)
    for buf, n in ((qs, 0), (dos, 1)):
        buf[0:HALO, :] = qd[n]
        buf[HALO:, :] = jnp.zeros((OWN - HALO, HDIM), BF16)
    first = lax.broadcasted_iota(jnp.int32, (1, TILE), 1) < BLOCK
    outside = jnp.where(chip == CHIPS - 1, NEG, 0.0)
    for t in range(OWN // TILE):
        cols = slice(t * TILE, (t + 1) * TILE)
        q_t = qs[cols, :]
        do_t = dos[cols, :]
        shift = outside - stat[0, 0:1, cols]
        delta = stat[0, 1:2, cols]
        for j in range(2 * t + 1, CHIP_BLOCKS):
            at = slice(j * BLOCK, (j + 1) * BLOCK)
            x = dot_nt(kx[at, :], q_t) * (SCALE * LOG2E) + shift
            if j == 2 * t + 1:
                x = jnp.where(first, x, NEG)
            p = jnp.exp2(x)
            dsb[at, cols] = (p * (dot_nt(vx[at, :], do_t) - delta)).astype(BF16)
            pb[at, cols] = p.astype(BF16)
    for j in range(0, CHIP_BLOCKS):
        at = slice(j * BLOCK, (j + 1) * BLOCK)
        upto = (j + 1) // 2 * TILE
        for n, (low, rows, by) in enumerate(((dsb, qs, SCALE), (pb, dos, 1.0))):
            value = dkv[n, at, :]
            if upto:
                value = value + dot_nn(low[at, :upto], rows[:upto, :])
            out[n, at, :] = value * by


def later(sc, off, own, recv, qd, stat, dkv):
    width = own.shape[2]
    heads = width // HDIM
    pair = pl.BlockSpec((2, OWN // 2, HDIM), lambda h, sc, off: (1, 0, h))
    full = pl.BlockSpec((2, OWN, HDIM), lambda h, sc, off: (0, 0, h))
    return pl.pallas_call(
        later_kernel,
        grid_spec=pltpu.PrefetchScalarGridSpec(
            num_scalar_prefetch=2,
            grid=(heads,),
            in_specs=[
                pair,
                pair,
                pl.BlockSpec((2, HALO, HDIM), lambda h, sc, off: (0, 0, h)),
                pl.BlockSpec((1, 8, OWN), lambda h, sc, off: (h, 0, 0)),
                full,
            ],
            out_specs=full,
            scratch_shapes=[pltpu.VMEM((OWN, HDIM), BF16)] * 4 + [pltpu.VMEM((OWN, OWN), BF16)] * 2,
        ),
        out_shape=jax.ShapeDtypeStruct((2, OWN, width), F32),
        compiler_params=params(),
        cost_estimate=cost(heads * 28 * 8 * 128**3 * 2, heads * 4_000_000),
        name="later",
    )(sc, off, own, recv, qd, stat, dkv)


def attn(sc, off, own, recv, halo, sums):
    width = own.shape[2]
    heads = width // HDIM
    keys = EXT + NSUM * BLOCK

    def by_head(n, rows):
        return pl.BlockSpec((n, rows, HDIM), lambda h, sc, off: (0, 0, h))

    sum_spec = pl.BlockSpec((2, BLOCK, HDIM), lambda h, sc, off: (0, 0, h))
    return pl.pallas_call(
        attn_kernel,
        grid_spec=pltpu.PrefetchScalarGridSpec(
            num_scalar_prefetch=2,
            grid=(heads,),
            in_specs=[by_head(4, OWN // 2), by_head(4, OWN // 2), by_head(2, HALO)]
            + [sum_spec] * NSUM,
            out_specs=[
                pl.BlockSpec((OWN, HDIM), lambda h, sc, off: (0, h)),
                by_head(2, OWN),
                pl.BlockSpec((1, 8, OWN), lambda h, sc, off: (h, 0, 0)),
                by_head(2, NSUM * BLOCK),
            ],
            scratch_shapes=[
                pltpu.VMEM((keys, HDIM), BF16),
                pltpu.VMEM((keys, HDIM), BF16),
                pltpu.VMEM((OWN, HDIM), BF16),
                pltpu.VMEM((OWN, HDIM), BF16),
                pltpu.VMEM((HDIM, keys), BF16),
                pltpu.VMEM((ROWS, TILE), F32),
                pltpu.VMEM((ROWS, TILE), F32),
                pltpu.VMEM((keys, OWN), BF16),
                pltpu.VMEM((OWN + NSUM * BLOCK, OWN), BF16),
            ],
        ),
        out_shape=[
            jax.ShapeDtypeStruct((OWN, width), BF16),
            jax.ShapeDtypeStruct((2, OWN, width), F32),
            jax.ShapeDtypeStruct((heads, 8, OWN), F32),
            jax.ShapeDtypeStruct((2, NSUM * BLOCK, width), BF16),
        ],
        compiler_params=params(),
        cost_estimate=cost(heads * 96 * 10 * 128**3 * 2, heads * 4_000_000),
        name="attn",
    )(sc, off, own, recv, halo, *sums)


def finish_kernel(sc, off, dq, dkv, *refs):
    tots, outs = refs[:SIDE], refs[SIDE:]
    core, y, z, x = sc[1], sc[2], sc[3], sc[4]
    local = off[y] & 7
    here = (off[y] >> 3) == z
    total = tots[0][...].astype(F32)
    for part in tots[1:]:
        total = total + part[...].astype(F32)
    for step in range(SIDE):
        for side in range(2):
            block = ((core + side) & 1) * SIDE + ((x + step) & 3)
            rows = pl.ds(pl.multiple_of(block * BLOCK, BLOCK), BLOCK)
            value = dkv[:, rows, :] + jnp.where(here & (local == block), total, 0.0)
            outs[step][side, 0] = dq[rows, :]
            outs[step][side, 1:3] = value.astype(BF16)


def finish(sc, off, dq, dkv, tots):
    width = dq.shape[1]
    shape = (2, 3, BLOCK, width)
    return pl.pallas_call(
        finish_kernel,
        grid_spec=pltpu.PrefetchScalarGridSpec(
            num_scalar_prefetch=2,
            grid=(width // HDIM,),
            in_specs=[
                pl.BlockSpec((OWN, HDIM), lambda h, sc, off: (0, h)),
                pl.BlockSpec((2, OWN, HDIM), lambda h, sc, off: (0, 0, h)),
            ]
            + [pl.BlockSpec((2, BLOCK, HDIM), lambda h, sc, off: (0, 0, h))] * SIDE,
            out_specs=[pl.BlockSpec((2, 3, BLOCK, HDIM), lambda h, sc, off: (0, 0, 0, h))] * SIDE,
        ),
        out_shape=[jax.ShapeDtypeStruct(shape, BF16)] * SIDE,
        compiler_params=params(),
        cost_estimate=cost(0, 20 * OWN * width),
        name="finish",
    )(sc, off, dq, dkv, *tots)


def place_kernel(sc, off, *refs):
    groups = len(SIZES)
    outs = refs[(SIDE + 1) * groups :]
    x, core = sc[4], sc[1]
    heads = sum(SIZES)
    at = 0
    for g in range(groups):
        width = SIZES[g] * HDIM
        for step in range(SIDE):
            source = (x + SIDE - step) & 3
            for part in range(2):
                side = core if part == 0 else 1 - core
                first = pl.multiple_of(((source * 2 + side) * heads + at) * HDIM, HDIM)
                ref = refs[g * (SIDE + 1) + (step if part == 0 else SIDE)]
                for n in range(3):
                    outs[n][:, pl.ds(first, width)] = ref[0 if part == 0 else step, n]
        at += SIZES[g]


def place(sc, off, parts):
    columns = sum(SIZES) * HDIM * 2 * SIDE
    shape = (BLOCK, columns)
    specs = []
    for n, p in enumerate(parts):
        lead = SIDE if n % (SIDE + 1) == SIDE else 1
        specs.append(pl.BlockSpec((lead, *p.shape[1:]), lambda i, sc, off: (0, 0, 0, 0)))
    return pl.pallas_call(
        place_kernel,
        grid_spec=pltpu.PrefetchScalarGridSpec(
            num_scalar_prefetch=2,
            grid=(1,),
            in_specs=specs,
            out_specs=[whole(shape)] * 3,
        ),
        out_shape=[jax.ShapeDtypeStruct(shape, BF16)] * 3,
        compiler_params=params(),
        cost_estimate=cost(0, 12 * BLOCK * columns),
        name="place",
    )(sc, off, *parts)


def named(value, pairs, axis="ctx"):
    return lax.ppermute(value, axis, pairs)


def on_device(query, key_in, value_in, dout, off):
    width = query.shape[1]
    me = lax.axis_index("ctx")
    x = lax.axis_index("tp")
    which = lax.iota(jnp.int32, 8)
    sc = jnp.where(which == 0, me >> 1, me & 1)
    sc = jnp.where(which == 2, me >> 3, sc)
    sc = jnp.where(which == 3, (me >> 1) & 3, sc)
    sc = jnp.where(which == 4, x, sc).astype(jnp.int32)
    y, z = me >> 3, (me >> 1) & 3

    own_cand, oth_cand = candidate(sc, off, key_in, value_in)
    pieces = pieces_of(sc, off, own_cand, named(oth_cand, SWAP))
    arrived = [pieces[0]]
    arrived += [named(pieces[n], along_z(n)) for n in range(1, SIDE)]
    step = (z - (off[y] >> 3)) & 3
    piece = arrived[0]
    for n in range(1, SIDE):
        piece = jnp.where(step == n, arrived[n], piece)
    parts = [piece] + [named(piece, along_z(n)) for n in range(1, SIDE)]
    summary = gather(sc, off, parts)

    bases = [sum(SIZES[:g]) for g in range(len(SIZES))]
    work = []
    for g, heads in enumerate(SIZES):
        own, oth = pack(sc, off, (query, dout, key_in, value_in), bases[g], heads, width)
        recv = named(oth, SWAP)
        qd, kv = halo_of(sc, off, own, recv)
        work.append((own, recv, named(kv, ring(1)), named(qd, ring(-1))))

    parts = []
    for g, heads in enumerate(SIZES):
        own, recv, kv, qd = work[g]
        mine = summary[:, :, bases[g] * HDIM : (bases[g] + heads) * HDIM]
        sums = [mine] + [named(mine, along_y(n)) for n in range(1, NSUM)]
        dq, dkv, stat, sent = attn(sc, off, own, recv, kv, sums)
        stat = named(stat, ring(-1))
        dkv = later(sc, off, own, recv, qd, stat, dkv)
        part = sent[:, :BLOCK].astype(F32)
        for n in range(1, NSUM):
            moved = named(sent[:, n * BLOCK : (n + 1) * BLOCK], along_y(-n))
            part = part + moved.astype(F32)
        part = part.astype(BF16)
        tots = [part] + [named(part, along_z(n)) for n in range(1, SIDE)]
        cuts = finish(sc, off, dq, dkv, tots)
        there = [cuts[0]]
        there += [named(cuts[n], along_x(n), "tp") for n in range(1, SIDE)]
        parts += there
        parts.append(named(jnp.concatenate([t[1:] for t in there], axis=0), SWAP))
    return tuple(place(sc, off, parts))


def solution(mesh):
    return jax.shard_map(
        on_device,
        mesh=mesh,
        in_specs=(P("ctx", "tp"), P("ctx", "tp"), P("ctx", "tp"), P("ctx", "tp"), P()),
        out_specs=(P(("ctx", "tp"), None),) * 3,
        check_vma=False,
    )
```

```python
import functools
import math

import jax
import jax.numpy as jnp
from jax import lax
from jax.experimental import pallas as pl
from jax.experimental.pallas import tpu as pltpu
from jax.sharding import PartitionSpec as P


HDIM = 128
BLOCK = 128
BAND = 8
STRIDE = 32
CHIP_BLOCKS = 8
HALO = (BAND - 1) * BLOCK
OWN = CHIP_BLOCKS * BLOCK
EXT = HALO + OWN
TILE = 256
NSUM = 4
SPAN = 9
ROWS = (SPAN + NSUM) * BLOCK
NEG = -1e30
SIZES = (3, 3)
CHIPS = 16
SIDE = 4
SCALE = HDIM**-0.5
LOG2E = math.log2(math.e)
BF16 = jnp.bfloat16
F32 = jnp.float32


def ring(step):
    return [(2 * c + k, 2 * ((c + step) % CHIPS) + k) for c in range(CHIPS) for k in range(2)]


def along_z(step):
    return [
        (2 * (y * SIDE + z) + k, 2 * (y * SIDE + (z + step) % SIDE) + k)
        for y in range(SIDE)
        for z in range(SIDE)
        for k in range(2)
    ]


def along_y(step):
    return [
        (2 * (y * SIDE + z) + k, 2 * ((y + step) % SIDE * SIDE + z) + k)
        for y in range(SIDE)
        for z in range(SIDE)
        for k in range(2)
    ]


SWAP = [(d, d ^ 1) for d in range(2 * CHIPS)]


def along_x(step):
    return [(x, (x + step) % SIDE) for x in range(SIDE)]


def params(**kw):
    return pltpu.CompilerParams(vmem_limit_bytes=56 * 1024 * 1024, **kw)


def cost(flops, nbytes):
    return pl.CostEstimate(flops=flops, bytes_accessed=nbytes, transcendentals=0)


def whole(shape):
    return pl.BlockSpec(shape, lambda *_: (0,) * len(shape))


def pack_kernel(sc, off, *refs):
    ins, (own, oth) = refs[:8], refs[8:]
    for n in range(4):
        own[n] = ins[2 * n][...]
        oth[n] = ins[2 * n + 1][...]


def pack(sc, off, arrays, base, heads, width):
    rows = arrays[0].shape[0]
    half = width // HDIM // 2
    chunk = 256
    cols = heads * HDIM
    specs, args = [], []
    for array in arrays:
        for other in (0, 1):
            specs.append(
                pl.BlockSpec(
                    (chunk, cols),
                    lambda i, sc, off, other=other: (
                        i,
                        jnp.abs(sc[1] - other) * (half // heads) + base // heads,
                    ),
                )
            )
            args.append(array)
    out = pl.BlockSpec((4, chunk, cols), lambda i, sc, off: (0, i, 0))
    shape = jax.ShapeDtypeStruct((4, rows, cols), BF16)
    return pl.pallas_call(
        pack_kernel,
        grid_spec=pltpu.PrefetchScalarGridSpec(
            num_scalar_prefetch=2,
            grid=(rows // chunk,),
            in_specs=specs,
            out_specs=[out, out],
        ),
        out_shape=[shape, shape],
        compiler_params=params(),
        cost_estimate=cost(0, 16 * rows * cols * 2),
        name="pack",
    )(sc, off, *args)


def halo_kernel(sc, off, own, recv, qd, kv):
    lo = OWN // 2

    def fill(first, second):
        @pl.when(pl.program_id(0) < 2)
        def _():
            qd[:, :lo] = first[...]
            qd[:, lo:] = second[:, : lo - BLOCK]

        @pl.when(pl.program_id(0) >= 2)
        def _():
            kv[:, : lo - BLOCK] = first[:, BLOCK:]
            kv[:, lo - BLOCK :] = second[...]

    pl.when(sc[1] == 0)(lambda: fill(own, recv))
    pl.when(sc[1] == 1)(lambda: fill(recv, own))


def halo_of(sc, off, own, recv):
    width = own.shape[2]
    spec = pl.BlockSpec((1, OWN // 2, width), lambda i, sc, off: (i, 0, 0))
    return pl.pallas_call(
        halo_kernel,
        grid_spec=pltpu.PrefetchScalarGridSpec(
            num_scalar_prefetch=2,
            grid=(4,),
            in_specs=[spec, spec],
            out_specs=[
                pl.BlockSpec((1, HALO, width), lambda i, sc, off: (jnp.minimum(i, 1), 0, 0)),
                pl.BlockSpec((1, HALO, width), lambda i, sc, off: (jnp.maximum(i - 2, 0), 0, 0)),
            ],
        ),
        out_shape=[jax.ShapeDtypeStruct((2, HALO, width), BF16)] * 2,
        compiler_params=params(),
        cost_estimate=cost(0, 16 * OWN * width * 2),
        name="halo",
    )(sc, off, own, recv)


def candidate_kernel(sc, off, key, value, own, oth):
    half = own.shape[2]
    for n, ref in enumerate((key, value)):
        own[n] = ref[:, pl.ds(pl.multiple_of(sc[1] * half, HDIM), half)]
        oth[n] = ref[:, pl.ds(pl.multiple_of((1 - sc[1]) * half, HDIM), half)]


def candidate(sc, off, key, value):
    width = key.shape[1]
    spec = pl.BlockSpec((BLOCK, width), lambda i, sc, off: (off[sc[2]] & 3, 0))
    shape = (2, BLOCK, width // 2)
    return pl.pallas_call(
        candidate_kernel,
        grid_spec=pltpu.PrefetchScalarGridSpec(
            num_scalar_prefetch=2, grid=(1,), in_specs=[spec] * 2, out_specs=[whole(shape)] * 2
        ),
        out_shape=[jax.ShapeDtypeStruct(shape, BF16)] * 2,
        compiler_params=params(),
        cost_estimate=cost(0, 8 * BLOCK * width),
        name="candidate",
    )(sc, off, key, value)


def pieces_kernel(sc, off, own, recv, *outs):
    piece = BLOCK // SIDE
    mine = ((off[sc[2]] & 7) >> 2) == sc[1]
    for step in range(SIDE):
        row = pl.multiple_of(((sc[3] + step) & 3) * piece, piece)

        def put(ref, out=outs[step], row=row):
            out[...] = ref[:, pl.ds(row, piece), :]

        pl.when(mine)(functools.partial(put, own))
        pl.when(jnp.logical_not(mine))(functools.partial(put, recv))


def pieces_of(sc, off, own, recv):
    shape = (2, BLOCK // SIDE, own.shape[2])
    return pl.pallas_call(
        pieces_kernel,
        grid_spec=pltpu.PrefetchScalarGridSpec(
            num_scalar_prefetch=2,
            grid=(1,),
            in_specs=[whole(own.shape)] * 2,
            out_specs=[whole(shape)] * SIDE,
        ),
        out_shape=[jax.ShapeDtypeStruct(shape, BF16)] * SIDE,
        compiler_params=params(),
        cost_estimate=cost(0, 8 * own.size),
        name="pieces",
    )(sc, off, own, recv)


def gather_kernel(sc, off, *refs):
    out = refs[SIDE]
    piece = BLOCK // SIDE
    for step in range(SIDE):
        row = pl.multiple_of(((sc[3] + SIDE - step) % SIDE) * piece, piece)
        out[:, pl.ds(row, piece), :] = refs[step][...]


def gather(sc, off, pieces):
    shape = pieces[0].shape
    full = (2, BLOCK, shape[2])
    return pl.pallas_call(
        gather_kernel,
        grid_spec=pltpu.PrefetchScalarGridSpec(
            num_scalar_prefetch=2, grid=(1,), in_specs=[whole(shape)] * SIDE, out_specs=whole(full)
        ),
        out_shape=jax.ShapeDtypeStruct(full, BF16),
        compiler_params=params(),
        cost_estimate=cost(0, 4 * BLOCK * shape[2] * 2),
        name="gather",
    )(sc, off, *pieces)


def fold(x, op):
    return op(x.reshape(x.shape[0] // 8, 8, x.shape[1]), axis=0)


def spread(x):
    return x.reshape(x.shape[0] // 8, 8, x.shape[1])


def dot_nt(a, b):
    return lax.dot_general(a, b, (((1,), (1,)), ((), ())), preferred_element_type=F32)


def dot_nn(a, b):
    return lax.dot_general(a, b, (((1,), (0,)), ((), ())), preferred_element_type=F32)


def load_own(buf, own, recv, core, n, start):
    half = OWN // 2
    buf[pl.ds(pl.multiple_of(start + core * half, BLOCK), half), :] = own[n]
    buf[pl.ds(pl.multiple_of(start + (1 - core) * half, BLOCK), half), :] = recv[n]


def attn_kernel(sc, off, own, recv, halo, s0, s1, s2, s3, dq, dkv, stat, ds_out, *scratch):
    kx, vx, qs, dos, kxt, xs, dps, dsb, pb = scratch
    core, chip, y = sc[1], sc[0], sc[2]
    load_own(qs, own, recv, core, 0, 0)
    load_own(dos, own, recv, core, 1, 0)
    for buf, n in ((kx, 0), (vx, 1)):
        buf[0:HALO, :] = halo[n]
        load_own(buf, own, recv, core, 2 + n, HALO)
        for s, part in enumerate((s0, s1, s2, s3)):
            buf[EXT + s * BLOCK : EXT + (s + 1) * BLOCK, :] = part[n]
    kxt[...] = kx[...].T
    row = lax.broadcasted_iota(jnp.int32, (BLOCK, TILE), 0)
    col = lax.broadcasted_iota(jnp.int32, (BLOCK, TILE), 1)
    first = lax.broadcasted_iota(jnp.int32, (1, TILE), 1) < BLOCK
    outside = jnp.where(chip == 0, NEG, 0.0)

    for t in range(OWN // TILE):
        base = t * TILE
        q_t = qs[base : base + TILE, :]
        do_t = dos[base : base + TILE, :]

        def start_of(j, base=base):
            return base + j * BLOCK if j < SPAN else EXT + (j - SPAN) * BLOCK

        m8 = jnp.full((8, TILE), NEG, F32)
        l8 = jnp.zeros((8, TILE), F32)
        d8 = jnp.zeros((8, TILE), F32)
        tops = []
        for j in range(SPAN + NSUM):
            span = slice(j * BLOCK, (j + 1) * BLOCK)
            at = slice(start_of(j), start_of(j) + BLOCK)
            x = dot_nt(kx[at, :], q_t) * (SCALE * LOG2E)
            if start_of(j) < HALO:
                x = x + outside
            if j == 0:
                x = jnp.where(first, x, NEG)
            if j == BAND - 1:
                x = jnp.where(row <= col, x, NEG)
            if j == BAND:
                x = jnp.where(row + BLOCK <= col, x, NEG)
            if j >= SPAN:
                slot = (y + NSUM - (j - SPAN)) & 3
                g = slot * STRIDE + off[slot]
                block = chip * CHIP_BLOCKS + 2 * t - (BAND - 1)
                b0 = jnp.where(g < block, 0.0, NEG)
                b1 = jnp.where(g < block + 1, 0.0, NEG)
                x = x + jnp.where(first, b0, b1)
            dp = dot_nt(vx[at, :], do_t)
            top = jnp.maximum(m8, fold(x, jnp.max))
            fade = jnp.exp2(m8 - top)
            p = jnp.exp2(spread(x) - top[None])
            l8 = l8 * fade + jnp.sum(p, axis=0)
            d8 = d8 * fade + jnp.sum(p * spread(dp), axis=0)
            xs[span, :] = p.reshape(BLOCK, TILE)
            dps[span, :] = dp
            m8 = top
            tops.append(top)
        m = jnp.max(m8, axis=0, keepdims=True)
        rest = jnp.exp2(m8 - m)
        total = jnp.sum(l8 * rest, axis=0, keepdims=True)
        inv = 1.0 / total
        delta = jnp.sum(d8 * rest, axis=0, keepdims=True) * inv
        stat[0, 0:1, base : base + TILE] = m + jnp.log2(total)
        stat[0, 1:2, base : base + TILE] = delta
        for j in range(SPAN + NSUM):
            span = slice(j * BLOCK, (j + 1) * BLOCK)
            factor = jnp.exp2(tops[j] - m) * inv
            p = (spread(xs[span, :]) * factor[None]).reshape(BLOCK, TILE)
            at = start_of(j)
            cols = slice(base, base + TILE)
            dsb[at : at + BLOCK, cols] = (p * (dps[span, :] - delta)).astype(BF16)
            if at >= HALO:
                pb[at - HALO : at - HALO + BLOCK, cols] = p.astype(BF16)
        cols = slice(base, base + TILE)
        dqt = dot_nn(kxt[:, base : base + SPAN * BLOCK], dsb[base : base + SPAN * BLOCK, cols])
        dqt = dqt + dot_nn(kxt[:, EXT:], dsb[EXT:, cols])
        dq[base : base + TILE, :] = (dqt * SCALE).T.astype(BF16)

    for t in range(OWN // TILE):
        keys = slice(t * TILE, (t + 1) * TILE)
        dkv[0, keys, :] = dot_nn(dsb[HALO + t * TILE : HALO + (t + 1) * TILE, t * TILE :], qs[t * TILE :, :])
        dkv[1, keys, :] = dot_nn(pb[keys, t * TILE :], dos[t * TILE :, :])
    for s in range(NSUM // 2):
        keys = slice(s * TILE, (s + 1) * TILE)
        ds_out[0, keys, :] = (
            dot_nn(dsb[EXT + s * TILE : EXT + (s + 1) * TILE, :], qs[...]) * SCALE
        ).astype(BF16)
        ds_out[1, keys, :] = dot_nn(pb[OWN + s * TILE : OWN + (s + 1) * TILE, :], dos[...]).astype(BF16)


def later_kernel(sc, off, own, recv, qd, stat, dkv, out, kx, vx, qs, dos, dsb, pb):
    core, chip = sc[1], sc[0]
    load_own(kx, own, recv, core, 0, 0)
    load_own(vx, own, recv, core, 1, 0)
    for buf, n in ((qs, 0), (dos, 1)):
        buf[0:HALO, :] = qd[n]
        buf[HALO:, :] = jnp.zeros((OWN - HALO, HDIM), BF16)
    first = lax.broadcasted_iota(jnp.int32, (1, TILE), 1) < BLOCK
    outside = jnp.where(chip == CHIPS - 1, NEG, 0.0)
    for t in range(OWN // TILE):
        cols = slice(t * TILE, (t + 1) * TILE)
        q_t = qs[cols, :]
        do_t = dos[cols, :]
        shift = outside - stat[0, 0:1, cols]
        delta = stat[0, 1:2, cols]
        for j in range(2 * t + 1, CHIP_BLOCKS):
            at = slice(j * BLOCK, (j + 1) * BLOCK)
            x = dot_nt(kx[at, :], q_t) * (SCALE * LOG2E) + shift
            if j == 2 * t + 1:
                x = jnp.where(first, x, NEG)
            p = jnp.exp2(x)
            dsb[at, cols] = (p * (dot_nt(vx[at, :], do_t) - delta)).astype(BF16)
            pb[at, cols] = p.astype(BF16)
    for j in range(0, CHIP_BLOCKS):
        at = slice(j * BLOCK, (j + 1) * BLOCK)
        upto = (j + 1) // 2 * TILE
        for n, (low, rows, by) in enumerate(((dsb, qs, SCALE), (pb, dos, 1.0))):
            value = dkv[n, at, :]
            if upto:
                value = value + dot_nn(low[at, :upto], rows[:upto, :])
            out[n, at, :] = value * by


def later(sc, off, own, recv, qd, stat, dkv):
    width = own.shape[2]
    heads = width // HDIM
    pair = pl.BlockSpec((2, OWN // 2, HDIM), lambda h, sc, off: (1, 0, h))
    full = pl.BlockSpec((2, OWN, HDIM), lambda h, sc, off: (0, 0, h))
    return pl.pallas_call(
        later_kernel,
        grid_spec=pltpu.PrefetchScalarGridSpec(
            num_scalar_prefetch=2,
            grid=(heads,),
            in_specs=[
                pair,
                pair,
                pl.BlockSpec((2, HALO, HDIM), lambda h, sc, off: (0, 0, h)),
                pl.BlockSpec((1, 8, OWN), lambda h, sc, off: (h, 0, 0)),
                full,
            ],
            out_specs=full,
            scratch_shapes=[pltpu.VMEM((OWN, HDIM), BF16)] * 4 + [pltpu.VMEM((OWN, OWN), BF16)] * 2,
        ),
        out_shape=jax.ShapeDtypeStruct((2, OWN, width), F32),
        compiler_params=params(),
        cost_estimate=cost(heads * 28 * 8 * 128**3 * 2, heads * 4_000_000),
        name="later",
    )(sc, off, own, recv, qd, stat, dkv)


def attn(sc, off, own, recv, halo, sums):
    width = own.shape[2]
    heads = width // HDIM
    keys = EXT + NSUM * BLOCK

    def by_head(n, rows):
        return pl.BlockSpec((n, rows, HDIM), lambda h, sc, off: (0, 0, h))

    sum_spec = pl.BlockSpec((2, BLOCK, HDIM), lambda h, sc, off: (0, 0, h))
    return pl.pallas_call(
        attn_kernel,
        grid_spec=pltpu.PrefetchScalarGridSpec(
            num_scalar_prefetch=2,
            grid=(heads,),
            in_specs=[by_head(4, OWN // 2), by_head(4, OWN // 2), by_head(2, HALO)]
            + [sum_spec] * NSUM,
            out_specs=[
                pl.BlockSpec((OWN, HDIM), lambda h, sc, off: (0, h)),
                by_head(2, OWN),
                pl.BlockSpec((1, 8, OWN), lambda h, sc, off: (h, 0, 0)),
                by_head(2, NSUM * BLOCK),
            ],
            scratch_shapes=[
                pltpu.VMEM((keys, HDIM), BF16),
                pltpu.VMEM((keys, HDIM), BF16),
                pltpu.VMEM((OWN, HDIM), BF16),
                pltpu.VMEM((OWN, HDIM), BF16),
                pltpu.VMEM((HDIM, keys), BF16),
                pltpu.VMEM((ROWS, TILE), F32),
                pltpu.VMEM((ROWS, TILE), F32),
                pltpu.VMEM((keys, OWN), BF16),
                pltpu.VMEM((OWN + NSUM * BLOCK, OWN), BF16),
            ],
        ),
        out_shape=[
            jax.ShapeDtypeStruct((OWN, width), BF16),
            jax.ShapeDtypeStruct((2, OWN, width), F32),
            jax.ShapeDtypeStruct((heads, 8, OWN), F32),
            jax.ShapeDtypeStruct((2, NSUM * BLOCK, width), BF16),
        ],
        compiler_params=params(),
        cost_estimate=cost(heads * 96 * 10 * 128**3 * 2, heads * 4_000_000),
        name="attn",
    )(sc, off, own, recv, halo, *sums)


def finish_kernel(sc, off, dkv, *refs):
    tots, rest = refs[:SIDE], refs[SIDE:]
    dqs, outs = rest[:-SIDE], rest[-SIDE:]
    lead = len(dqs)
    core, y, z, x = sc[1], sc[2], sc[3], sc[4]
    local = off[y] & 7
    here = (off[y] >> 3) == z
    total = tots[0][...].astype(F32)
    for part in tots[1:]:
        total = total + part[...].astype(F32)
    for step in range(SIDE):
        for side in range(2):
            block = ((core + side) & 1) * SIDE + ((x + step) & 3)
            rows = pl.ds(pl.multiple_of(block * BLOCK, BLOCK), BLOCK)
            value = dkv[:, rows, :] + jnp.where(here & (local == block), total, 0.0)
            for dq in dqs:
                outs[step][side, 0] = dq[rows, :]
            outs[step][side, lead : lead + 2] = value.astype(BF16)


def finish(sc, off, dkv, tots, dqs=()):
    width = dkv.shape[2]
    shape = (2, 2 + len(dqs), BLOCK, width)
    return pl.pallas_call(
        finish_kernel,
        grid_spec=pltpu.PrefetchScalarGridSpec(
            num_scalar_prefetch=2,
            grid=(width // HDIM,),
            in_specs=[
                pl.BlockSpec((2, OWN, HDIM), lambda h, sc, off: (0, 0, h)),
            ]
            + [pl.BlockSpec((2, BLOCK, HDIM), lambda h, sc, off: (0, 0, h))] * SIDE
            + [pl.BlockSpec((OWN, HDIM), lambda h, sc, off: (0, h))] * len(dqs),
            out_specs=[pl.BlockSpec((*shape[:3], HDIM), lambda h, sc, off: (0, 0, 0, h))] * SIDE,
        ),
        out_shape=[jax.ShapeDtypeStruct(shape, BF16)] * SIDE,
        compiler_params=params(),
        cost_estimate=cost(0, 20 * OWN * width),
        name="finish",
    )(sc, off, dkv, *tots, *dqs)


def cut_kernel(sc, off, dq, *outs):
    core, x = sc[1], sc[4]
    for step in range(SIDE):
        for side in range(2):
            block = ((core + side) & 1) * SIDE + ((x + step) & 3)
            rows = pl.ds(pl.multiple_of(block * BLOCK, BLOCK), BLOCK)
            outs[step][side, 0] = dq[rows, :]


def cut(sc, off, dq):
    shape = (2, 1, BLOCK, dq.shape[1])
    return pl.pallas_call(
        cut_kernel,
        grid_spec=pltpu.PrefetchScalarGridSpec(
            num_scalar_prefetch=2,
            grid=(1,),
            in_specs=[whole(dq.shape)],
            out_specs=[whole(shape)] * SIDE,
        ),
        out_shape=[jax.ShapeDtypeStruct(shape, BF16)] * SIDE,
        compiler_params=params(),
        cost_estimate=cost(0, 4 * OWN * shape[3]),
        name="cut",
    )(sc, off, dq)


def place_kernel(slots, sc, off, *refs):
    groups = len(SIZES)
    outs = refs[(SIDE + 1) * groups :]
    x, core = sc[4], sc[1]
    heads = sum(SIZES)
    at = 0
    for g in range(groups):
        width = SIZES[g] * HDIM
        for step in range(SIDE):
            source = (x + SIDE - step) & 3
            for part in range(2):
                side = core if part == 0 else 1 - core
                first = pl.multiple_of(((source * 2 + side) * heads + at) * HDIM, HDIM)
                ref = refs[g * (SIDE + 1) + (step if part == 0 else SIDE)]
                for n, out in enumerate(outs):
                    out[:, pl.ds(first, width)] = ref[0 if part == 0 else step, slots[g] + n]
        at += SIZES[g]


def place(sc, off, parts, count, slots):
    columns = sum(SIZES) * HDIM * 2 * SIDE
    shape = (BLOCK, columns)
    specs = []
    for n, p in enumerate(parts):
        lead = SIDE if n % (SIDE + 1) == SIDE else 1
        used = min(p.shape[1], slots[n // (SIDE + 1)] + count)
        specs.append(pl.BlockSpec((lead, used, *p.shape[2:]), lambda i, sc, off: (0, 0, 0, 0)))
    return pl.pallas_call(
        functools.partial(place_kernel, slots),
        grid_spec=pltpu.PrefetchScalarGridSpec(
            num_scalar_prefetch=2,
            grid=(1,),
            in_specs=specs,
            out_specs=[whole(shape)] * count,
        ),
        out_shape=[jax.ShapeDtypeStruct(shape, BF16)] * count,
        compiler_params=params(),
        cost_estimate=cost(0, 4 * count * BLOCK * columns),
        name="place",
    )(sc, off, *parts)


def spread_out(cuts):
    there = [cuts[0]]
    there += [named(cuts[n], along_x(n), "tp") for n in range(1, SIDE)]
    return there + [named(jnp.concatenate([t[1:] for t in there], axis=0), SWAP)]


def named(value, pairs, axis="ctx"):
    return lax.ppermute(value, axis, pairs)


def on_device(query, key_in, value_in, dout, off):
    width = query.shape[1]
    me = lax.axis_index("ctx")
    x = lax.axis_index("tp")
    which = lax.iota(jnp.int32, 8)
    sc = jnp.where(which == 0, me >> 1, me & 1)
    sc = jnp.where(which == 2, me >> 3, sc)
    sc = jnp.where(which == 3, (me >> 1) & 3, sc)
    sc = jnp.where(which == 4, x, sc).astype(jnp.int32)
    y, z = me >> 3, (me >> 1) & 3

    own_cand, oth_cand = candidate(sc, off, key_in, value_in)
    pieces = pieces_of(sc, off, own_cand, named(oth_cand, SWAP))
    arrived = [pieces[0]]
    arrived += [named(pieces[n], along_z(n)) for n in range(1, SIDE)]
    step = (z - (off[y] >> 3)) & 3
    piece = arrived[0]
    for n in range(1, SIDE):
        piece = jnp.where(step == n, arrived[n], piece)
    parts = [piece] + [named(piece, along_z(n)) for n in range(1, SIDE)]
    summary = gather(sc, off, parts)

    bases = [sum(SIZES[:g]) for g in range(len(SIZES))]
    work = []
    for g, heads in enumerate(SIZES):
        own, oth = pack(sc, off, (query, dout, key_in, value_in), bases[g], heads, width)
        recv = named(oth, SWAP)
        qd, kv = halo_of(sc, off, own, recv)
        work.append((own, recv, named(kv, ring(1)), named(qd, ring(-1))))

    dqs, dkvs, totals = [], [], []
    for g, heads in enumerate(SIZES):
        own, recv, kv, qd = work[g]
        mine = summary[:, :, bases[g] * HDIM : (bases[g] + heads) * HDIM]
        sums = [mine] + [named(mine, along_y(n)) for n in range(1, NSUM)]
        dq, dkv, stat, sent = attn(sc, off, own, recv, kv, sums)
        stat = named(stat, ring(-1))
        dkv = later(sc, off, own, recv, qd, stat, dkv)
        part = sent[:, :BLOCK].astype(F32)
        for n in range(1, NSUM):
            moved = named(sent[:, n * BLOCK : (n + 1) * BLOCK], along_y(-n))
            part = part + moved.astype(F32)
        part = part.astype(BF16)
        totals.append([part] + [named(part, along_z(n)) for n in range(1, SIDE)])
        dqs.append(dq)
        dkvs.append(dkv)
    cuts = cut(sc, off, dqs[0])
    first_q = spread_out(cuts)
    cuts = finish(sc, off, dkvs[0], totals[0], (dqs[1],))
    mixed = spread_out(cuts)
    cuts = finish(sc, off, dkvs[1], totals[1])
    last = spread_out(cuts)
    grad_q = place(sc, off, first_q + mixed, 1, (0, 0))
    grads = place(sc, off, mixed + last, 2, (1, 0))
    return (*grad_q, *grads)


def solution(mesh):
    return jax.shard_map(
        on_device,
        mesh=mesh,
        in_specs=(P("ctx", "tp"), P("ctx", "tp"), P("ctx", "tp"), P("ctx", "tp"), P()),
        out_specs=(P(("ctx", "tp"), None),) * 3,
        check_vma=False,
    )
```
